32 devices in a mesh: dp: 8 (over y, x, core), seq: 4 (over z).
Axes of the slice: x: 2, y: 2, z: 4, core: 2. Of those that a mesh axis runs over, the one named last changes fastest.
Arguments:
- layer_input: bfloat16 [16, 1024, 1536], P('dp', 'seq'), may hold values from -6 to 6
- attn_gain: bfloat16 [1536], P('dp'), may hold values from 0.099609375 to 1.8984375
- query_weight: bfloat16 [1536, 1536], P('dp'), may hold values from -0.15625 to 0.15625
- key_matrix: bfloat16 [1536, 768], P('dp'), may hold values from -0.15625 to 0.15625
- value_matrix: bfloat16 [1536, 768], P('dp'), may hold values from -0.15625 to 0.15625
- output_weight: bfloat16 [1536, 1536], P('dp'), may hold values from -2.5 to 2.5
- ffn_gain: bfloat16 [1536], P('dp'), may hold values from 0.099609375 to 1.8984375
- gate_weight: bfloat16 [1536, 4096], P('dp'), may hold values from -0.15625 to 0.15625
- up_weight: bfloat16 [1536, 4096], P('dp'), may hold values from -0.15625 to 0.15625
- down_weight: bfloat16 [4096, 1536], P('dp'), may hold values from -0.09375 to 0.09375
- cotangent: bfloat16 [16, 1024, 1536], P('dp', 'seq'), may hold values from -6 to 6
Outputs:
- layer_output: bfloat16 [16, 1024, 1536], P('dp', 'seq')
- input_grad: float32 [16, 1024, 1536], P('dp', 'seq')
- attn_gain_grad: float32 [1536], P('dp')
- query_weight_grad: float32 [1536, 1536], P('dp')
- key_weight_grad: float32 [1536, 768], P('dp')
- value_weight_grad: float32 [1536, 768], P('dp')
- output_weight_grad: float32 [1536, 1536], P('dp')
- ffn_gain_grad: float32 [1536], P('dp')
- gate_weight_grad: float32 [1536, 4096], P('dp')
- up_weight_grad: float32 [1536, 4096], P('dp')
- down_weight_grad: float32 [4096, 1536], P('dp')
The draws below stay inside these ranges and needn't reach their ends.
All inputs are finite; a program needn't handle non-finite values.
Results may differ from the reference program's by a relative error of at most 0.019.
Values may be sent and summed in bfloat16 or wider, within the bound.
No kernel may reach another device: no remote copies, remote signals or barrier semaphores. Data moves between devices by JAX's collectives and lax.ppermute only.
A program may use at most 320 MiB of HBM per device.

```python
import jax
import jax.numpy as jnp
from jax import lax

MODEL_WIDTH = 1536
QUERY_HEADS = 16
KEY_VALUE_HEADS = 8
HEAD_SIZE = 96
HIDDEN_UNITS = 4096
SEQUENCE_TOKENS = 1024
SEQS = 16


def shard_levels(key, dims, shards, least, high):
    def one(position, parts):
        draws = jax.random.uniform(jax.random.fold_in(jax.random.fold_in(key, 6), position), (parts,), jnp.float32, least / len(shards), high / len(shards))
        return jnp.repeat(jnp.exp(draws), dims[position] // parts).reshape((-1,) + (1,) * (len(dims) - position - 1))

    level = one(*shards[0])
    for cut in shards[1:]:
        level = level * one(*cut)
    return level


def scatter_about(stream_key, extent, deviation, reach, cuts=(), kind=jnp.bfloat16):
    entries = jax.random.normal(stream_key, extent, jnp.float32) * deviation
    if len(cuts) > 0:
        entries = shard_levels(stream_key, extent, cuts, -0.22, 0.18) * entries
    return jnp.clip(entries, min=-reach, max=reach).astype(kind)


def setup_inputs(seed: int = 0) -> dict:
    streams_of = jax.random.split(jax.random.key(seed), 12)
    layer_input = scatter_about(streams_of[0], (SEQS, SEQUENCE_TOKENS, MODEL_WIDTH), 1.0, 6.0, ((0, 8), (1, 4)))
    attn_gain = jnp.clip(1.0 + 0.18 * jax.random.normal(streams_of[1], (MODEL_WIDTH,), jnp.float32), 0.099609375, 1.8984375).astype(jnp.bfloat16)
    query_weight = scatter_about(streams_of[2], (MODEL_WIDTH, QUERY_HEADS * HEAD_SIZE), MODEL_WIDTH ** -0.5, 0.15625, ((0, 8),))
    key_matrix = scatter_about(streams_of[3], (MODEL_WIDTH, KEY_VALUE_HEADS * HEAD_SIZE), MODEL_WIDTH ** -0.5, 0.15625, ((0, 8),))
    value_matrix = scatter_about(streams_of[4], (MODEL_WIDTH, KEY_VALUE_HEADS * HEAD_SIZE), MODEL_WIDTH ** -0.5, 0.15625, ((0, 8),))
    output_weight = scatter_about(streams_of[5], (QUERY_HEADS * HEAD_SIZE, MODEL_WIDTH), (max(1, QUERY_HEADS * HEAD_SIZE * 4 // SEQUENCE_TOKENS)) ** -0.5, 2.5, ((0, 8),))
    ffn_gain = jnp.clip(1.0 + 0.18 * jax.random.normal(streams_of[6], (MODEL_WIDTH,), jnp.float32), 0.099609375, 1.8984375).astype(jnp.bfloat16)
    gate_weight = scatter_about(streams_of[7], (MODEL_WIDTH, HIDDEN_UNITS), MODEL_WIDTH ** -0.5, 0.15625, ((0, 8),))
    up_weight = scatter_about(streams_of[8], (MODEL_WIDTH, HIDDEN_UNITS), MODEL_WIDTH ** -0.5, 0.15625, ((0, 8),))
    down_weight = scatter_about(streams_of[9], (HIDDEN_UNITS, MODEL_WIDTH), HIDDEN_UNITS ** -0.5, 0.09375, ((0, 8),))
    cotangent = scatter_about(streams_of[10], (SEQS, SEQUENCE_TOKENS, MODEL_WIDTH), 1.0, 6.0, ((0, 8), (1, 4)))
    return dict(layer_input=layer_input, attn_gain=attn_gain, query_weight=query_weight, key_matrix=key_matrix, value_matrix=value_matrix, output_weight=output_weight, ffn_gain=ffn_gain, gate_weight=gate_weight, up_weight=up_weight, down_weight=down_weight, cotangent=cotangent)


eps = 1e-06
theta_base = 100000.0

def rope_tables(count, start_offset, width):
    half = width // 2
    freq = theta_base ** (-(jnp.arange(half).astype(jnp.float32) * 2.0) / width)
    places = (start_offset + jnp.arange(count)).astype(jnp.float32)
    angle = places[:, None] * freq[None, :]
    angle = jnp.concatenate([angle, angle], axis=1)
    return (jnp.cos(angle), jnp.sin(angle))

def rotate(field):
    half = field.shape[-1] // 2
    return jnp.concatenate([-field[..., half:], field[..., :half]], axis=-1)

def rope_forward(field, cosine_table, sine_table):
    return field * cosine_table + rotate(field) * sine_table

def rotary_backward(field, cosine_table, sine_table):
    return field * cosine_table - rotate(field) * sine_table

def norm_backward(grad_norm, unit, gain, inverse):
    scaled = grad_norm * gain
    return inverse * (scaled - unit * lax.optimization_barrier(jnp.mean(scaled * unit, axis=-1, keepdims=True)))

def reference(layer_input, attn_gain, query_weight, key_matrix, value_matrix, output_weight, ffn_gain, gate_weight, up_weight, down_weight, cotangent):
    scale = HEAD_SIZE ** (-0.5)
    query_group_count = QUERY_HEADS // KEY_VALUE_HEADS
    cosine_table, sine_table = rope_tables(SEQUENCE_TOKENS, 0, HEAD_SIZE)
    cosine_table = cosine_table[:, None, :]
    sine_table = sine_table[:, None, :]
    causal = jnp.arange(SEQUENCE_TOKENS)[:, None] >= jnp.arange(SEQUENCE_TOKENS)[None, :]
    gain_one = attn_gain.astype(jnp.float32)
    gain_two = ffn_gain.astype(jnp.float32)
    single_float = jnp.float32
    half_precision = jnp.bfloat16

    def one_sequence(totals, pair):
        inputs, upstream = pair
        resid_in = inputs.astype(single_float)
        inv_one = lax.rsqrt(lax.optimization_barrier(jnp.mean(resid_in * resid_in, axis=-1, keepdims=True)) + eps)
        unit_one = resid_in * inv_one
        first_normed = (unit_one * gain_one).astype(half_precision)
        query_rows = jnp.dot(first_normed, query_weight, preferred_element_type=single_float).reshape(SEQUENCE_TOKENS, QUERY_HEADS, HEAD_SIZE)
        key_rows = jnp.dot(first_normed, key_matrix, preferred_element_type=single_float).reshape(SEQUENCE_TOKENS, KEY_VALUE_HEADS, HEAD_SIZE)
        value_rows = jnp.dot(first_normed, value_matrix, preferred_element_type=single_float).reshape(SEQUENCE_TOKENS, KEY_VALUE_HEADS, HEAD_SIZE)
        query_rows = rope_forward(query_rows, cosine_table, sine_table).astype(half_precision)
        key_rows = rope_forward(key_rows, cosine_table, sine_table).astype(half_precision)
        value_rows = value_rows.astype(half_precision)
        keys_all = jnp.tile(key_rows, (1, query_group_count, 1))
        values_all = jnp.tile(value_rows, (1, query_group_count, 1))
        scores = jnp.einsum('qhd,khd->hqk', query_rows.astype(single_float), keys_all.astype(single_float)) * scale
        masked = jnp.where(causal, scores, -1e+30)
        peak = lax.optimization_barrier(jnp.max(masked, axis=-1, keepdims=True))
        logsum = peak + jnp.log(lax.optimization_barrier(jnp.sum(jnp.exp(masked - peak), axis=-1, keepdims=True)))
        probs = jnp.where(causal, jnp.exp(scores - logsum), 0.0)
        probs_half = probs.astype(half_precision)
        attended = jnp.einsum('hqk,khd->qhd', probs_half.astype(single_float), values_all.astype(single_float)).astype(half_precision)
        flat_att = attended.reshape(SEQUENCE_TOKENS, QUERY_HEADS * HEAD_SIZE)
        resid_mid = resid_in + jnp.dot(flat_att, output_weight, preferred_element_type=single_float)
        inv_two = lax.rsqrt(lax.optimization_barrier(jnp.mean(resid_mid * resid_mid, axis=-1, keepdims=True)) + eps)
        unit_two = resid_mid * inv_two
        normed_two = (unit_two * gain_two).astype(half_precision)
        gate = jnp.dot(normed_two, gate_weight, preferred_element_type=single_float)
        upward = jnp.dot(normed_two, up_weight, preferred_element_type=single_float)
        sigma = jax.nn.sigmoid(gate)
        silu_gate = gate * sigma
        hidden = (silu_gate * upward).astype(half_precision)
        layer_out = (resid_mid + jnp.dot(hidden, down_weight, preferred_element_type=single_float)).astype(half_precision)
        grad_hidden = jnp.dot(upstream, down_weight.T, preferred_element_type=single_float)
        down_grad = jnp.dot(hidden.T, upstream, preferred_element_type=single_float)
        grad_gate = (grad_hidden * upward * sigma * (1.0 + gate * (1.0 - sigma))).astype(half_precision)
        grad_up = (grad_hidden * silu_gate).astype(half_precision)
        gate_grad = jnp.dot(normed_two.T, grad_gate, preferred_element_type=single_float)
        up_grad = jnp.dot(normed_two.T, grad_up, preferred_element_type=single_float)
        grad_norm_two = jnp.dot(grad_gate, gate_weight.T, preferred_element_type=single_float) + jnp.dot(grad_up, up_weight.T, preferred_element_type=single_float)
        ffn_gain_grad = lax.optimization_barrier(jnp.sum(grad_norm_two * unit_two, axis=0))
        grad_mid = upstream.astype(single_float) + norm_backward(grad_norm_two, unit_two, gain_two, inv_two)
        grad_mid_half = grad_mid.astype(half_precision)
        out_grad = jnp.dot(flat_att.T, grad_mid_half, preferred_element_type=single_float)
        grad_att = jnp.dot(grad_mid_half, output_weight.T, preferred_element_type=single_float).astype(half_precision).reshape(SEQUENCE_TOKENS, QUERY_HEADS, HEAD_SIZE)
        grad_probs = jnp.einsum('qhd,khd->hqk', grad_att.astype(single_float), values_all.astype(single_float))
        delta = lax.optimization_barrier(jnp.sum(grad_att.astype(single_float) * attended.astype(single_float), axis=-1))
        grad_scores = (probs * (grad_probs - delta.T[:, :, None])).astype(half_precision)
        grad_queries = jnp.einsum('hqk,khd->qhd', grad_scores.astype(single_float), keys_all.astype(single_float)) * scale
        key_gradient_total = jnp.einsum('hqk,qhd->khd', grad_scores.astype(single_float), query_rows.astype(single_float)) * scale
        value_gradient_total = jnp.einsum('hqk,qhd->khd', probs_half.astype(single_float), grad_att.astype(single_float))
        key_gradient = lax.optimization_barrier(jnp.sum(key_gradient_total.reshape(SEQUENCE_TOKENS, query_group_count, KEY_VALUE_HEADS, HEAD_SIZE), axis=1))
        value_gradient = lax.optimization_barrier(jnp.sum(value_gradient_total.reshape(SEQUENCE_TOKENS, query_group_count, KEY_VALUE_HEADS, HEAD_SIZE), axis=1))
        queries_back = rotary_backward(grad_queries, cosine_table, sine_table).astype(half_precision).reshape(SEQUENCE_TOKENS, QUERY_HEADS * HEAD_SIZE)
        key_rows_restored = rotary_backward(key_gradient, cosine_table, sine_table).astype(half_precision).reshape(SEQUENCE_TOKENS, KEY_VALUE_HEADS * HEAD_SIZE)
        value_rows_restored = value_gradient.astype(half_precision).reshape(SEQUENCE_TOKENS, KEY_VALUE_HEADS * HEAD_SIZE)
        query_grad = jnp.dot(first_normed.T, queries_back, preferred_element_type=single_float)
        key_grad = jnp.dot(first_normed.T, key_rows_restored, preferred_element_type=single_float)
        value_grad = jnp.dot(first_normed.T, value_rows_restored, preferred_element_type=single_float)
        grad_norm_one = jnp.dot(queries_back, query_weight.T, preferred_element_type=single_float)
        grad_norm_one = grad_norm_one + jnp.dot(key_rows_restored, key_matrix.T, preferred_element_type=single_float)
        grad_norm_one = grad_norm_one + jnp.dot(value_rows_restored, value_matrix.T, preferred_element_type=single_float)
        attn_gain_grad = lax.optimization_barrier(jnp.sum(grad_norm_one * unit_one, axis=0))
        input_grad = grad_mid + norm_backward(grad_norm_one, unit_one, gain_one, inv_one)
        terms = (attn_gain_grad, query_grad, key_grad, value_grad, out_grad, ffn_gain_grad, gate_grad, up_grad, down_grad)
        totals = tuple((total + term for total, term in zip(totals, terms)))
        return (totals, (layer_out, input_grad))
    start_offset = (jnp.zeros((MODEL_WIDTH,), jnp.float32), jnp.zeros((MODEL_WIDTH, QUERY_HEADS * HEAD_SIZE), jnp.float32), jnp.zeros((MODEL_WIDTH, KEY_VALUE_HEADS * HEAD_SIZE), jnp.float32), jnp.zeros((MODEL_WIDTH, KEY_VALUE_HEADS * HEAD_SIZE), jnp.float32), jnp.zeros((QUERY_HEADS * HEAD_SIZE, MODEL_WIDTH), jnp.float32), jnp.zeros((MODEL_WIDTH,), jnp.float32), jnp.zeros((MODEL_WIDTH, HIDDEN_UNITS), jnp.float32), jnp.zeros((MODEL_WIDTH, HIDDEN_UNITS), jnp.float32), jnp.zeros((HIDDEN_UNITS, MODEL_WIDTH), jnp.float32))
    totals, stacked = lax.scan(one_sequence, start_offset, (layer_input, cotangent))
    layer_output, input_grad = stacked
    return (layer_output, input_grad, totals[0], totals[1], totals[2], totals[3], totals[4], totals[5], totals[6], totals[7], totals[8])
```

```python
import jax
import jax.numpy as jnp
from jax import lax
from jax.experimental import pallas as pl
from jax.experimental.pallas import tpu as pltpu
from jax.sharding import PartitionSpec as P

QUERY_HEADS = 16
KEY_VALUE_HEADS = 8
HEAD_SIZE = 96


eps = 1e-06
theta_base = 100000.0


def rope_tables(count, start_offset, width):
    half = width // 2
    freq = theta_base ** (-(jnp.arange(half).astype(jnp.float32) * 2.0) / width)
    places = (start_offset + jnp.arange(count)).astype(jnp.float32)
    angle = places[:, None] * freq[None, :]
    angle = jnp.concatenate([angle, angle], axis=1)
    return (jnp.cos(angle), jnp.sin(angle))


def rotate(field):
    half = field.shape[-1] // 2
    return jnp.concatenate([-field[..., half:], field[..., :half]], axis=-1)


def rope_forward(field, cosine_table, sine_table):
    return field * cosine_table + rotate(field) * sine_table


def rotary_backward(field, cosine_table, sine_table):
    return field * cosine_table - rotate(field) * sine_table


def norm_backward(grad_norm, unit, gain, inverse):
    scaled = grad_norm * gain
    return inverse * (scaled - unit * jnp.mean(scaled * unit, axis=-1, keepdims=True))


def times_transposed(left, right):
    return lax.dot_general(
        left, right, (((1,), (1,)), ((), ())), preferred_element_type=jnp.float32
    )


def transposed_times(left, right):
    return lax.dot_general(
        left, right, (((0,), (0,)), ((), ())), preferred_element_type=jnp.float32
    )


def block_probs(query_block, key_block, start_offset, logsum_block):
    block = query_block.shape[1]
    stop = key_block.shape[1]
    scores = jnp.einsum(
        "sqgcd,skcd->sgcqk", query_block, key_block, preferred_element_type=jnp.float32
    ) * HEAD_SIZE ** (-0.5)
    causal = (start_offset + jnp.arange(block))[:, None] >= jnp.arange(stop)[None, :]
    if logsum_block is None:
        masked = jnp.where(causal, scores, -1e30)
        peak = jnp.max(masked, axis=-1, keepdims=True)
        logsum_block = peak + jnp.log(jnp.sum(jnp.exp(masked - peak), axis=-1, keepdims=True))
    probs = jnp.where(causal, jnp.exp(scores - logsum_block), 0.0)
    return (probs, logsum_block)


def body(
    layer_input,
    attn_gain,
    query_weight,
    key_matrix,
    value_matrix,
    output_weight,
    ffn_gain,
    gate_weight,
    up_weight,
    down_weight,
    cotangent,
):
    sequence_count, local_length, width = layer_input.shape
    token_rows = sequence_count * local_length
    shard_count = lax.axis_size("seq")
    length = local_length * shard_count
    query_group_count = QUERY_HEADS // KEY_VALUE_HEADS
    local_key_value = KEY_VALUE_HEADS // shard_count
    scale = HEAD_SIZE ** (-0.5)
    half_precision = jnp.bfloat16
    query_all, key_all, value_all, output_all, gain_one = (
        lax.all_gather(query_weight, "dp", axis=0, tiled=True),
        lax.all_gather(key_matrix, "dp", axis=0, tiled=True),
        lax.all_gather(value_matrix, "dp", axis=0, tiled=True),
        lax.all_gather(output_weight, "dp", axis=0, tiled=True),
        lax.all_gather(attn_gain, "dp", axis=0, tiled=True),
    )
    gate_all, up_all, down_all, gain_two = (
        lax.all_gather(gate_weight, "dp", axis=0, tiled=True),
        lax.all_gather(up_weight, "dp", axis=0, tiled=True),
        lax.all_gather(down_weight, "dp", axis=0, tiled=True),
        lax.all_gather(ffn_gain, "dp", axis=0, tiled=True),
    )
    gain_one = gain_one.astype(jnp.float32)
    gain_two = gain_two.astype(jnp.float32)
    resid_in = layer_input.reshape(token_rows, width).astype(jnp.float32)
    inv_one = lax.rsqrt(jnp.mean(resid_in * resid_in, axis=-1, keepdims=True) + eps)
    unit_one = resid_in * inv_one
    first_normed = (unit_one * gain_one).astype(half_precision)
    cosine_table, sine_table = rope_tables(
        local_length, lax.axis_index("seq") * local_length, HEAD_SIZE
    )
    query_rows = jnp.dot(first_normed, query_all, preferred_element_type=jnp.float32).reshape(
        sequence_count, local_length, QUERY_HEADS, HEAD_SIZE
    )
    key_rows = jnp.dot(first_normed, key_all, preferred_element_type=jnp.float32).reshape(
        sequence_count, local_length, KEY_VALUE_HEADS, HEAD_SIZE
    )
    value_rows = jnp.dot(first_normed, value_all, preferred_element_type=jnp.float32)
    query_rows = rope_forward(query_rows, cosine_table[:, None, :], sine_table[:, None, :]).astype(
        half_precision
    )
    key_rows = rope_forward(key_rows, cosine_table[:, None, :], sine_table[:, None, :]).astype(
        half_precision
    )
    query_rows = query_rows.reshape(
        sequence_count, local_length, query_group_count, KEY_VALUE_HEADS * HEAD_SIZE
    )
    paired = jnp.stack(
        [
            key_rows.reshape(sequence_count, local_length, KEY_VALUE_HEADS * HEAD_SIZE),
            value_rows.astype(half_precision).reshape(
                sequence_count, local_length, KEY_VALUE_HEADS * HEAD_SIZE
            ),
        ],
        axis=2,
    )
    query_heads, pair_heads = (
        lax.all_to_all(query_rows, "seq", split_axis=3, concat_axis=1, tiled=True),
        lax.all_to_all(paired, "seq", split_axis=3, concat_axis=1, tiled=True),
    )
    query_heads = query_heads.reshape(
        sequence_count, length, query_group_count, local_key_value, HEAD_SIZE
    )
    key_heads = pair_heads[:, :, 0].reshape(sequence_count, length, local_key_value, HEAD_SIZE)
    value_heads = pair_heads[:, :, 1].reshape(sequence_count, length, local_key_value, HEAD_SIZE)
    block = min(512, length)
    count = length // block
    attended_blocks = []
    logsums = []
    for index in range(count):
        start_offset = index * block
        stop = start_offset + block
        probs, logsum_block = block_probs(
            query_heads[:, start_offset:stop], key_heads[:, :stop], start_offset, None
        )
        logsums.append(logsum_block)
        probs_half = probs.astype(half_precision)
        attended_blocks.append(
            jnp.einsum(
                "sgcqk,skcd->sqgcd",
                probs_half,
                value_heads[:, :stop],
                preferred_element_type=jnp.float32,
            ).astype(half_precision)
        )
    attended_heads = jnp.concatenate(attended_blocks, axis=1)
    attended_tok = lax.all_to_all(
        attended_heads.reshape(
            sequence_count, length, query_group_count, local_key_value * HEAD_SIZE
        ),
        "seq",
        split_axis=1,
        concat_axis=3,
        tiled=True,
    )
    flat_att = attended_tok.reshape(token_rows, QUERY_HEADS * HEAD_SIZE)
    resid_mid = resid_in + jnp.dot(flat_att, output_all, preferred_element_type=jnp.float32)
    inv_two = lax.rsqrt(jnp.mean(resid_mid * resid_mid, axis=-1, keepdims=True) + eps)
    unit_two = resid_mid * inv_two
    normed_two = (unit_two * gain_two).astype(half_precision)
    gate = jnp.dot(normed_two, gate_all, preferred_element_type=jnp.float32)
    upward = jnp.dot(normed_two, up_all, preferred_element_type=jnp.float32)
    sigma = jax.nn.sigmoid(gate)
    silu_gate = gate * sigma
    hidden = (silu_gate * upward).astype(half_precision)
    layer_output = (
        resid_mid + jnp.dot(hidden, down_all, preferred_element_type=jnp.float32)
    ).astype(half_precision)
    upstream = cotangent.reshape(token_rows, width)
    grad_hidden = times_transposed(upstream, down_all)
    down_grad = transposed_times(hidden, upstream)
    grad_gate = (grad_hidden * upward * sigma * (1.0 + gate * (1.0 - sigma))).astype(half_precision)
    grad_up = (grad_hidden * silu_gate).astype(half_precision)
    gate_grad = transposed_times(normed_two, grad_gate)
    up_grad = transposed_times(normed_two, grad_up)
    grad_norm_two = times_transposed(grad_gate, gate_all) + times_transposed(grad_up, up_all)
    ffn_gain_grad = jnp.sum(grad_norm_two * unit_two, axis=0)
    gate_grad, up_grad, down_grad, ffn_gain_grad = (
        lax.psum_scatter(
            gate_grad.astype(jnp.bfloat16), "dp", scatter_dimension=0, tiled=True
        ).astype(jnp.float32),
        lax.psum_scatter(
            up_grad.astype(jnp.bfloat16), "dp", scatter_dimension=0, tiled=True
        ).astype(jnp.float32),
        lax.psum_scatter(
            down_grad.astype(jnp.bfloat16), "dp", scatter_dimension=0, tiled=True
        ).astype(jnp.float32),
        lax.psum_scatter(
            ffn_gain_grad.astype(jnp.bfloat16), "dp", scatter_dimension=0, tiled=True
        ).astype(jnp.float32),
    )
    gate_grad, up_grad, down_grad, ffn_gain_grad = (
        lax.psum(gate_grad.astype(jnp.bfloat16), "seq").astype(jnp.float32),
        lax.psum(up_grad.astype(jnp.bfloat16), "seq").astype(jnp.float32),
        lax.psum(down_grad.astype(jnp.bfloat16), "seq").astype(jnp.float32),
        lax.psum(ffn_gain_grad.astype(jnp.bfloat16), "seq").astype(jnp.float32),
    )
    grad_mid = upstream.astype(jnp.float32) + norm_backward(
        grad_norm_two, unit_two, gain_two, inv_two
    )
    grad_mid_half = grad_mid.astype(half_precision)
    out_grad = transposed_times(flat_att, grad_mid_half)
    grad_att = (
        times_transposed(grad_mid_half, output_all)
        .astype(half_precision)
        .reshape(sequence_count, local_length, query_group_count, KEY_VALUE_HEADS * HEAD_SIZE)
    )
    grad_heads = lax.all_to_all(grad_att, "seq", split_axis=3, concat_axis=1, tiled=True)
    grad_heads = grad_heads.reshape(
        sequence_count, length, query_group_count, local_key_value, HEAD_SIZE
    )
    query_grad_blocks = []
    key_gradient = jnp.zeros((sequence_count, length, local_key_value, HEAD_SIZE), jnp.float32)
    value_gradient = jnp.zeros((sequence_count, length, local_key_value, HEAD_SIZE), jnp.float32)
    for index in range(count):
        start_offset = index * block
        stop = start_offset + block
        query_block = query_heads[:, start_offset:stop]
        key_block = key_heads[:, :stop]
        value_block = value_heads[:, :stop]
        grad_block = grad_heads[:, start_offset:stop]
        probs, unused = block_probs(query_block, key_block, start_offset, logsums[index])
        probs_half = probs.astype(half_precision)
        grad_probs = jnp.einsum(
            "sqgcd,skcd->sgcqk", grad_block, value_block, preferred_element_type=jnp.float32
        )
        delta = jnp.sum(
            grad_block.astype(jnp.float32)
            * attended_heads[:, start_offset:stop].astype(jnp.float32),
            axis=-1,
        )
        delta = jnp.transpose(delta, (0, 2, 3, 1))[..., None]
        grad_scores = (probs * (grad_probs - delta)).astype(half_precision)
        query_grad_blocks.append(
            jnp.einsum(
                "sgcqk,skcd->sqgcd", grad_scores, key_block, preferred_element_type=jnp.float32
            )
            * scale
        )
        key_part = (
            jnp.einsum(
                "sgcqk,sqgcd->skcd", grad_scores, query_block, preferred_element_type=jnp.float32
            )
            * scale
        )
        value_part = jnp.einsum(
            "sgcqk,sqgcd->skcd", probs_half, grad_block, preferred_element_type=jnp.float32
        )
        padding = ((0, 0), (0, length - stop), (0, 0), (0, 0))
        key_gradient = key_gradient + jnp.pad(key_part, padding)
        value_gradient = value_gradient + jnp.pad(value_part, padding)
    grad_queries = jnp.concatenate(query_grad_blocks, axis=1)
    cos_full, sin_full = rope_tables(length, 0, HEAD_SIZE)
    queries_back = rotary_backward(
        grad_queries, cos_full[:, None, None, :], sin_full[:, None, None, :]
    ).astype(half_precision)
    key_rows_restored = rotary_backward(
        key_gradient, cos_full[:, None, :], sin_full[:, None, :]
    ).astype(half_precision)
    value_rows_restored = value_gradient.astype(half_precision)
    queries_back = queries_back.reshape(
        sequence_count, length, query_group_count, local_key_value * HEAD_SIZE
    )
    pair_back = jnp.stack(
        [
            key_rows_restored.reshape(sequence_count, length, local_key_value * HEAD_SIZE),
            value_rows_restored.reshape(sequence_count, length, local_key_value * HEAD_SIZE),
        ],
        axis=2,
    )
    queries_tok, paired_token_rows = (
        lax.all_to_all(queries_back, "seq", split_axis=1, concat_axis=3, tiled=True),
        lax.all_to_all(pair_back, "seq", split_axis=1, concat_axis=3, tiled=True),
    )
    queries_tok = queries_tok.reshape(token_rows, QUERY_HEADS * HEAD_SIZE)
    key_token_rows = paired_token_rows[:, :, 0].reshape(token_rows, KEY_VALUE_HEADS * HEAD_SIZE)
    value_token_rows = paired_token_rows[:, :, 1].reshape(token_rows, KEY_VALUE_HEADS * HEAD_SIZE)
    query_grad = transposed_times(first_normed, queries_tok)
    key_grad = transposed_times(first_normed, key_token_rows)
    value_grad = transposed_times(first_normed, value_token_rows)
    grad_norm_one = (
        times_transposed(queries_tok, query_all)
        + times_transposed(key_token_rows, key_all)
        + times_transposed(value_token_rows, value_all)
    )
    attn_gain_grad = jnp.sum(grad_norm_one * unit_one, axis=0)
    query_grad, key_grad, value_grad, out_grad, attn_gain_grad = (
        lax.psum_scatter(
            query_grad.astype(jnp.bfloat16), "dp", scatter_dimension=0, tiled=True
        ).astype(jnp.float32),
        lax.psum_scatter(
            key_grad.astype(jnp.bfloat16), "dp", scatter_dimension=0, tiled=True
        ).astype(jnp.float32),
        lax.psum_scatter(
            value_grad.astype(jnp.bfloat16), "dp", scatter_dimension=0, tiled=True
        ).astype(jnp.float32),
        lax.psum_scatter(
            out_grad.astype(jnp.bfloat16), "dp", scatter_dimension=0, tiled=True
        ).astype(jnp.float32),
        lax.psum_scatter(
            attn_gain_grad.astype(jnp.bfloat16), "dp", scatter_dimension=0, tiled=True
        ).astype(jnp.float32),
    )
    query_grad, key_grad, value_grad, out_grad, attn_gain_grad = (
        lax.psum(query_grad.astype(jnp.bfloat16), "seq").astype(jnp.float32),
        lax.psum(key_grad.astype(jnp.bfloat16), "seq").astype(jnp.float32),
        lax.psum(value_grad.astype(jnp.bfloat16), "seq").astype(jnp.float32),
        lax.psum(out_grad.astype(jnp.bfloat16), "seq").astype(jnp.float32),
        lax.psum(attn_gain_grad.astype(jnp.bfloat16), "seq").astype(jnp.float32),
    )
    input_grad = grad_mid + norm_backward(grad_norm_one, unit_one, gain_one, inv_one)
    return (
        layer_output.reshape(sequence_count, local_length, width),
        input_grad.reshape(sequence_count, local_length, width),
        attn_gain_grad,
        query_grad,
        key_grad,
        value_grad,
        out_grad,
        ffn_gain_grad,
        gate_grad,
        up_grad,
        down_grad,
    )


SAME_CORE = [[0, 2, 4, 6], [1, 3, 5, 7]]
VMEM_BYTES = 48 * 1024 * 1024


def flip(field, bit):
    count = lax.axis_size("dp")
    return lax.ppermute(field, "dp", [(i, i ^ bit) for i in range(count)])


def cross(field, bit):
    return lax.ppermute(field, "seq", [(i, i ^ bit) for i in range(4)])


def column_swap(field, turn, back):
    pairs = []
    for dp in range(8):
        for place in range(4):
            chip, core, high, low = dp // 2, dp % 2, place // 2, place % 2
            target = (2 * chip + (high ^ 1)) * 4 + 2 * core + (low ^ turn)
            pairs.append((target, dp * 4 + place) if back else (dp * 4 + place, target))
    return lax.ppermute(field, ("dp", "seq"), pairs)


def pick_order(swapped, first, second, axis=0):
    return jnp.where(
        swapped,
        jnp.concatenate([second, first], axis=axis),
        jnp.concatenate([first, second], axis=axis),
    )


def sequence_parts(field, low):
    return [
        column_swap(lax.dynamic_index_in_dim(field, low ^ turn, 0, keepdims=False), turn, False)
        for turn in range(2)
    ]


def slice_parts(half, low):
    rows = half.shape[0] // 2
    return [
        column_swap(lax.dynamic_slice_in_dim(half, (low ^ turn) * rows, rows, 0), turn, True)
        for turn in range(2)
    ]


def join_slices(parts, low):
    return jnp.where(low == 1, jnp.stack(parts[::-1]), jnp.stack(parts))


def both_cores(half, core):
    return pick_order(core == 0, half, flip(half, 1))


def relative_columns(field, chip):
    width = field.shape[-1] // 4
    return jnp.concatenate(
        [lax.dynamic_slice_in_dim(field, (chip ^ r) * width, width, field.ndim - 1) for r in range(4)],
        axis=-1,
    )


def gather_chips(block):
    half = block.shape[0] // 2
    from_x = flip(block, 2)
    from_y = flip(block, 4)
    corner_x = flip(from_y[:half], 2)
    corner_y = flip(from_x[half:], 4)
    return block, from_x, from_y, corner_x, corner_y


def add_half(*terms):
    total = terms[0].astype(jnp.float32)
    for term in terms[1:]:
        total = total + term.astype(jnp.float32)
    return total.astype(jnp.bfloat16)


def scatter_first(field):
    half = field.shape[0] // 8
    corner = field[6 * half :]
    return flip(corner[:half], 2), flip(corner[half:], 4)


def scatter_second(field, got_x, got_y):
    rows = field.shape[0] // 4
    half = rows // 2
    over_x, over_y = field[rows : 2 * rows], field[2 * rows : 3 * rows]
    send_x = jnp.concatenate([over_x[:half], add_half(over_x[half:], got_y)], axis=0)
    send_y = jnp.concatenate([add_half(over_y[:half], got_x), over_y[half:]], axis=0)
    return flip(send_x, 2), flip(send_y, 4)


def halve(field, bit_value, bit):
    size = field.shape[0] // 2
    own = lax.dynamic_slice_in_dim(field, bit_value * size, size, 0)
    other = lax.dynamic_slice_in_dim(field, (1 - bit_value) * size, size, 0)
    return add_half(own, cross(other, bit))


def join(field, bit_value, bit):
    return pick_order(bit_value == 1, field, cross(field, bit))


def prepare_kernel(core_ref, gate_mine, gate_theirs, up_mine, up_theirs, mine_ref, theirs_ref):
    for gate, up, out in ((gate_mine, up_mine, mine_ref), (gate_theirs, up_theirs, theirs_ref)):
        part = gate.shape[1] // 2
        for group in range(2):
            out[group, :, :part] = gate[:, group * part : (group + 1) * part]
            out[group, :, part:] = up[:, group * part : (group + 1) * part]


def prepare_ffn(gate_weight, up_weight, core):
    rows, columns = gate_weight.shape
    piece = columns // 8
    mine = pl.BlockSpec((rows, piece), lambda j, c: (0, 2 * j + c[0]))
    theirs = pl.BlockSpec((rows, piece), lambda j, c: (0, 2 * j + 1 - c[0]))
    out = pl.BlockSpec((2, rows, piece), lambda j, c: (0, 0, j))
    shape = jax.ShapeDtypeStruct((2, rows, columns // 2), jnp.bfloat16)
    return pl.pallas_call(
        prepare_kernel,
        out_shape=(shape, shape),
        grid_spec=pltpu.PrefetchScalarGridSpec(
            num_scalar_prefetch=1,
            grid=(4,),
            in_specs=[mine, theirs, mine, theirs],
            out_specs=(out, out),
        ),
        name="prepare_ffn",
    )(core.reshape(1), gate_weight, gate_weight, up_weight, up_weight)


def merge_kernel(core_ref, own_0, other_0, own_1, other_1, gate_ref, up_ref):
    part = own_0.shape[1] // 2
    mine = core_ref[0] == pl.program_id(1)
    first = jnp.where(mine, own_0[...].astype(jnp.float32), other_0[...].astype(jnp.float32))
    second = jnp.where(mine, own_1[...].astype(jnp.float32), other_1[...].astype(jnp.float32))
    gate_ref[:, :part] = first[:, :part]
    gate_ref[:, part:] = second[:, :part]
    up_ref[:, :part] = first[:, part:]
    up_ref[:, part:] = second[:, part:]


def merge_ffn(own_0, other_0, own_1, other_1, core):
    rows, columns = own_0.shape
    piece = columns // 4
    part = pl.BlockSpec((rows, piece), lambda j, i, c: (0, j))
    out = pl.BlockSpec((rows, piece), lambda j, i, c: (0, 2 * j + i))
    shape = jax.ShapeDtypeStruct((rows, columns * 2), jnp.float32)
    return pl.pallas_call(
        merge_kernel,
        out_shape=(shape, shape),
        grid_spec=pltpu.PrefetchScalarGridSpec(
            num_scalar_prefetch=1,
            grid=(4, 2),
            in_specs=[part] * 4,
            out_specs=(out, out),
        ),
        name="merge_ffn",
    )(core.reshape(1), own_0, other_0, own_1, other_1)


def hint(flops, bytes_accessed, transcendentals=0):
    return pl.CostEstimate(
        flops=flops // 8, transcendentals=transcendentals // 8, bytes_accessed=bytes_accessed // 8
    )


def stacked(pieces, rows):
    own, from_x, from_y, corner_x, corner_y = pieces
    rest = rows - corner_x.shape[0]
    return jnp.concatenate(
        [own[:rows, :], from_x[:rows, :], from_y[:rows, :], corner_x[...], corner_y[:rest, :]],
        axis=0,
    )


def hidden_kernel(rows, normed, upstream, *refs):
    down, hidden, grads = refs[5:]
    part = grads.shape[1] // 2
    weight = stacked(refs[:5], rows)
    tile = 256
    for start in range(0, normed.shape[0], tile):
        lines = pl.ds(start, tile)
        total = jnp.dot(normed[lines, :], weight, preferred_element_type=jnp.float32)
        grad_hidden = lax.dot_general(
            upstream[lines, :], down[...], (((1,), (1,)), ((), ())), preferred_element_type=jnp.float32
        )
        gate, upward = total[:, :part], total[:, part:]
        sigma = jax.nn.sigmoid(gate)
        silu_gate = gate * sigma
        hidden[lines, :] = (silu_gate * upward).astype(jnp.bfloat16)
        grads[lines, :part] = (
            grad_hidden * upward * sigma * (1.0 + gate * (1.0 - sigma))
        ).astype(jnp.bfloat16)
        grads[lines, part:] = (grad_hidden * silu_gate).astype(jnp.bfloat16)


def hidden_stage(normed, upstream, pieces, down):
    length, width = normed.shape
    columns = pieces[0].shape[1]
    piece = columns // 4
    whole = pl.BlockSpec((length, width), lambda j: (0, 0), pipeline_mode=pl.Buffered(1))
    return pl.pallas_call(
        lambda *refs: hidden_kernel(width // 4, *refs),
        out_shape=(
            jax.ShapeDtypeStruct((length, columns // 2), jnp.bfloat16),
            jax.ShapeDtypeStruct((length, columns), jnp.bfloat16),
        ),
        grid=(4,),
        in_specs=[whole, whole]
        + [pl.BlockSpec((p.shape[0], piece), lambda j: (0, j)) for p in pieces]
        + [pl.BlockSpec((piece // 2, width), lambda j: (j, 0))],
        out_specs=(
            pl.BlockSpec((length, piece // 2), lambda j: (0, j)),
            pl.BlockSpec((length, piece), lambda j: (0, j)),
        ),
        compiler_params=pltpu.CompilerParams(vmem_limit_bytes=VMEM_BYTES),
        cost_estimate=hint(
            3 * length * width * columns,
            4 * length * width + 3 * width * columns + 3 * length * columns,
            length * columns // 2,
        ),
        name="hidden_stage",
    )(normed, upstream, *pieces, down)


NEGATIVE = -1e30
LANES = 128


def turned(field, cos, sin_low, sin_high, sign):
    half = HEAD_SIZE // 2
    spun = pltpu.roll(field, LANES - half, 1) * sin_low + pltpu.roll(field, half, 1) * sin_high
    return field * cos + sign * spun


def project_kernel(rows, heads, normed, cos, sin_low, sin_high, *refs):
    out, weight = refs[5:]
    own, from_x, from_y, corner_x, corner_y = refs[:5]
    rest = rows - corner_x.shape[0]

    @pl.when(pl.program_id(0) == 0)
    def _():
        start = 0
        for piece, count in (
            (own, rows), (from_x, rows), (from_y, rows), (corner_x, rows - rest), (corner_y, rest)
        ):
            lines = pl.ds(start, count)
            for head in range(heads):
                weight[lines, pl.ds(head * LANES, HEAD_SIZE)] = piece[
                    :count, pl.ds(head * HEAD_SIZE, HEAD_SIZE)
                ]
                weight[lines, pl.ds(head * LANES + HEAD_SIZE, LANES - HEAD_SIZE)] = jnp.zeros(
                    (count, LANES - HEAD_SIZE), jnp.bfloat16
                )
            start += count

    part = jnp.dot(normed[...], weight[...], preferred_element_type=jnp.float32)
    for head in range(heads):
        columns = slice(head * LANES, (head + 1) * LANES)
        field = part[:, columns]
        if head < heads * 3 // 4:
            field = turned(field, cos[...], sin_low[...], sin_high[...], 1.0)
        out[:, columns] = field.astype(jnp.bfloat16)


def project_stage(normed, pieces, tables):
    length, width = normed.shape
    columns = pieces[0].shape[1]
    heads = columns // HEAD_SIZE
    tile = 256
    table = pl.BlockSpec((tile, LANES), lambda i: (i, 0))
    return pl.pallas_call(
        lambda *refs: project_kernel(width // 4, heads, *refs),
        out_shape=(
            jax.ShapeDtypeStruct((length, heads * LANES), jnp.bfloat16),
            jax.ShapeDtypeStruct((width, heads * LANES), jnp.bfloat16),
        ),
        grid=(length // tile,),
        in_specs=[pl.BlockSpec((tile, width), lambda i: (i, 0)), table, table, table]
        + [
            pl.BlockSpec(p.shape, lambda i: (0, 0), pipeline_mode=pl.Buffered(1)) for p in pieces
        ],
        out_specs=(
            pl.BlockSpec((tile, heads * LANES), lambda i: (i, 0)),
            pl.BlockSpec((width, heads * LANES), lambda i: (0, 0), pipeline_mode=pl.Buffered(1)),
        ),
        compiler_params=pltpu.CompilerParams(vmem_limit_bytes=VMEM_BYTES),
        cost_estimate=hint(
            2 * length * width * heads * LANES,
            2 * length * width + 4 * width * columns + 2 * length * columns,
        ),
        name="project_stage",
    )(normed, *tables, *pieces)


def block_softmax(query, key, tile, index):
    scale = HEAD_SIZE ** (-0.5)
    lines = pl.ds(index * tile, tile)
    before = index * tile

    def scores(which):
        return scale * lax.dot_general(
            query[lines, :], key[which, :], (((1,), (1,)), ((), ())),
            preferred_element_type=jnp.float32,
        )

    last = scores(lines)
    seen = lax.broadcasted_iota(jnp.int32, (tile, tile), 0) >= lax.broadcasted_iota(
        jnp.int32, (tile, tile), 1
    )
    last = jnp.where(seen, last, NEGATIVE)
    peak = jnp.max(last, axis=1, keepdims=True)
    if before:
        earlier = scores(pl.ds(0, before))
        peak = jnp.maximum(peak, jnp.max(earlier, axis=1, keepdims=True))
    last = jnp.exp(last - peak)
    total = jnp.sum(last, axis=1, keepdims=True)
    if before:
        earlier = jnp.exp(earlier - peak)
        total = total + jnp.sum(earlier, axis=1, keepdims=True)
    inverse = 1.0 / total
    parts = [(lines, last * inverse)]
    if before:
        parts.append((pl.ds(0, before), earlier * inverse))
    return lines, parts


def attention_kernel(tile, query, key, value, out):
    for index in range(query.shape[0] // tile):
        lines, parts = block_softmax(query, key, tile, index)
        total = 0.0
        for which, probs in parts:
            total = total + jnp.dot(
                probs.astype(jnp.bfloat16), value[which, :], preferred_element_type=jnp.float32
            )
        out[lines, :] = total.astype(jnp.bfloat16)


def attention_stage(fields, heads, kv_heads):
    length = fields.shape[0]
    tile = min(256, length)
    spec = lambda start, count: pl.BlockSpec((length, LANES), lambda h: (0, start + h % count))
    return pl.pallas_call(
        lambda *refs: attention_kernel(tile, *refs),
        out_shape=jax.ShapeDtypeStruct((length, heads * LANES), jnp.bfloat16),
        grid=(heads,),
        in_specs=[spec(0, heads), spec(heads, kv_heads), spec(heads + kv_heads, kv_heads)],
        out_specs=spec(0, heads),
        compiler_params=pltpu.CompilerParams(vmem_limit_bytes=VMEM_BYTES),
        cost_estimate=hint(
            2 * heads * length * length * LANES,
            6 * heads * length * LANES,
            heads * length * length // 2,
        ),
        name="attention_stage",
    )(fields, fields, fields)


def attention_back_kernel(tile, *refs):
    query_0, query_1, key, value, out_0, out_1, grad_0, grad_1 = refs[:8]
    cos, sin_low, sin_high, back_0, back_1, key_back, value_back, key_sum, value_sum = refs[8:]
    scale = HEAD_SIZE ** (-0.5)
    key_sum[...] = jnp.zeros_like(key_sum)
    value_sum[...] = jnp.zeros_like(value_sum)
    for query, out, grad, back in (
        (query_0, out_0, grad_0, back_0),
        (query_1, out_1, grad_1, back_1),
    ):
        for index in range(query.shape[0] // tile):
            lines, parts = block_softmax(query, key, tile, index)
            upstream = grad[lines, :]
            delta = jnp.sum(
                upstream.astype(jnp.float32) * out[lines, :].astype(jnp.float32),
                axis=1,
                keepdims=True,
            )
            total = 0.0
            for which, probs in parts:
                grad_probs = lax.dot_general(
                    upstream, value[which, :], (((1,), (1,)), ((), ())),
                    preferred_element_type=jnp.float32,
                )
                grad_scores = (probs * (grad_probs - delta)).astype(jnp.bfloat16)
                total = total + jnp.dot(
                    grad_scores, key[which, :], preferred_element_type=jnp.float32
                )
                key_sum[which, :] += lax.dot_general(
                    grad_scores, query[lines, :], (((0,), (0,)), ((), ())),
                    preferred_element_type=jnp.float32,
                )
                value_sum[which, :] += lax.dot_general(
                    probs.astype(jnp.bfloat16), upstream, (((0,), (0,)), ((), ())),
                    preferred_element_type=jnp.float32,
                )
            back[lines, :] = turned(
                total * scale, cos[lines, :], sin_low[lines, :], sin_high[lines, :], -1.0
            ).astype(jnp.bfloat16)
    key_back[...] = turned(
        key_sum[...] * scale, cos[...], sin_low[...], sin_high[...], -1.0
    ).astype(jnp.bfloat16)
    value_back[...] = value_sum[...].astype(jnp.bfloat16)


def attention_back_stage(fields, attended, grads, tables, kv_heads):
    length = fields.shape[0]
    tile = min(256, length)
    spec = lambda start: pl.BlockSpec((length, LANES), lambda h: (0, start + h))
    table = pl.BlockSpec((length, LANES), lambda h: (0, 0))
    shape = jax.ShapeDtypeStruct((length, kv_heads * LANES), jnp.bfloat16)
    first, second = spec(0), spec(kv_heads)
    return pl.pallas_call(
        lambda *refs: attention_back_kernel(tile, *refs),
        out_shape=(shape,) * 4,
        grid=(kv_heads,),
        in_specs=[first, second, spec(2 * kv_heads), spec(3 * kv_heads)]
        + [first, second] * 2
        + [table] * 3,
        out_specs=(first,) * 4,
        scratch_shapes=[pltpu.VMEM((length, LANES), jnp.float32)] * 2,
        compiler_params=pltpu.CompilerParams(vmem_limit_bytes=VMEM_BYTES),
        cost_estimate=hint(
            10 * kv_heads * length * length * LANES,
            30 * kv_heads * length * LANES,
            kv_heads * length * length,
        ),
        name="attention_back_stage",
    )(fields, fields, fields, fields, attended, attended, grads, grads, *tables)


def inputs_back_kernel(rows, chip_ref, *refs):
    weight, out = refs[-2:]
    columns = refs[0].shape[1]
    part = 0.0
    for j, grad in enumerate(refs[:-2]):
        part = part + lax.dot_general(
            grad[...], weight[:, j * columns : (j + 1) * columns], (((1,), (1,)), ((), ())),
            preferred_element_type=jnp.float32,
        )
    for r in range(4):
        where = pl.ds(pl.multiple_of((chip_ref[0] ^ r) * rows, 128), rows)
        out[:, where] = part[:, r * rows : (r + 1) * rows]


def inputs_back_stage(backs, weight, chip):
    length, columns = backs[0].shape
    width = weight.shape[0]
    tile = 256
    return pl.pallas_call(
        lambda *refs: inputs_back_kernel(width // 4, *refs),
        out_shape=jax.ShapeDtypeStruct((length, width), jnp.float32),
        grid_spec=pltpu.PrefetchScalarGridSpec(
            num_scalar_prefetch=1,
            grid=(length // tile,),
            in_specs=[pl.BlockSpec((tile, columns), lambda i, c: (i, 0))] * len(backs)
            + [pl.BlockSpec(weight.shape, lambda i, c: (0, 0), pipeline_mode=pl.Buffered(1))],
            out_specs=pl.BlockSpec((tile, width), lambda i, c: (i, 0)),
        ),
        compiler_params=pltpu.CompilerParams(vmem_limit_bytes=VMEM_BYTES),
        cost_estimate=hint(
            2 * length * width * weight.shape[1], 2 * width * weight.shape[1] + 8 * length * width
        ),
        name="inputs_back_stage",
    )(chip.reshape(1), *backs, weight)


def weight_kernel(normed, *refs):
    gains, out = refs[-2:]
    rows = normed.shape[1]
    heads = refs[0].shape[1] // LANES
    for j, back in enumerate(refs[:-2]):
        part = lax.dot_general(
            normed[...], back[...], (((0,), (0,)), ((), ())), preferred_element_type=jnp.float32
        ).astype(jnp.bfloat16)
        for head in range(heads):
            out[:rows, pl.ds((j * heads + head) * HEAD_SIZE, HEAD_SIZE)] = part[
                :, head * LANES : head * LANES + HEAD_SIZE
            ]
    out[rows:, :] = gains[...]


def weight_stage(normed, backs, gains):
    length, width = normed.shape
    columns = gains.shape[1]
    rows, extra = width // 4, gains.shape[0] // 4
    whole = pl.BlockSpec(backs[0].shape, lambda i: (0, 0), pipeline_mode=pl.Buffered(1))
    return pl.pallas_call(
        weight_kernel,
        out_shape=jax.ShapeDtypeStruct((width + 4 * extra, columns), jnp.bfloat16),
        grid=(4,),
        in_specs=[pl.BlockSpec((length, rows), lambda i: (0, i))]
        + [whole] * len(backs)
        + [pl.BlockSpec((extra, columns), lambda i: (i, 0))],
        out_specs=pl.BlockSpec((rows + extra, columns), lambda i: (i, 0)),
        compiler_params=pltpu.CompilerParams(vmem_limit_bytes=VMEM_BYTES),
        cost_estimate=hint(
            2 * length * width * columns,
            2 * length * width + 2 * width * columns + 2 * length * columns,
        ),
        name="weight_stage",
    )(normed, *backs, gains)


def back_kernel(rows, with_base, chip_ref, grads, *rest):
    weight, out = rest[-1], rest[-2]

    @pl.when(pl.program_id(0) == 0)
    def _():
        weight[...] = stacked(rest[:5], rows)

    part = lax.dot_general(
        grads[...], weight[...], (((1,), (1,)), ((), ())), preferred_element_type=jnp.float32
    )
    for r in range(4):
        columns = pl.ds(pl.multiple_of((chip_ref[0] ^ r) * rows, 128), rows)
        block = part[:, r * rows : (r + 1) * rows]
        if with_base:
            block = block + rest[5][:, columns]
        out[:, columns] = block


def back_stage(grads, pieces, chip, base=None):
    length, columns = grads.shape
    width = (pieces[0].shape[0] // 128 * 128) * 4
    tile = 256
    line = pl.BlockSpec((tile, width), lambda i, c: (i, 0))
    inputs = [grads, *pieces] + ([] if base is None else [base])
    return pl.pallas_call(
        lambda *refs: back_kernel(width // 4, base is not None, *refs),
        out_shape=jax.ShapeDtypeStruct((length, width), jnp.float32),
        grid_spec=pltpu.PrefetchScalarGridSpec(
            num_scalar_prefetch=1,
            grid=(length // tile,),
            in_specs=[pl.BlockSpec((tile, columns), lambda i, c: (i, 0))]
            + [
                pl.BlockSpec(p.shape, lambda i, c: (0, 0), pipeline_mode=pl.Buffered(1))
                for p in pieces
            ]
            + ([] if base is None else [line]),
            out_specs=line,
            scratch_shapes=[pltpu.VMEM((width, columns), jnp.bfloat16)],
        ),
        compiler_params=pltpu.CompilerParams(vmem_limit_bytes=VMEM_BYTES),
        cost_estimate=hint(
            2 * length * width * columns,
            2 * length * columns + 2 * width * columns + 4 * length * width,
        ),
        name="back_stage",
    )(chip.reshape(1), *inputs)


def split_cores(field, chips):
    piece = field.shape[1] // (2 * chips)
    cuts = [field[:, i * piece : (i + 1) * piece] for i in range(2 * chips)]
    return cuts[::2], cuts[1::2]


def interleave(own, other, chips, core):
    piece = own.shape[1] // chips
    parts = []
    for i in range(chips):
        a, b = own[:, i * piece : (i + 1) * piece], other[:, i * piece : (i + 1) * piece]
        parts += [jnp.where(core == 0, a, b), jnp.where(core == 0, b, a)]
    return jnp.concatenate(parts, axis=1).astype(jnp.float32)


def paired_body(
    layer_input,
    attn_gain,
    query_weight,
    key_matrix,
    value_matrix,
    output_weight,
    ffn_gain,
    gate_weight,
    up_weight,
    down_weight,
    cotangent,
):
    f32, bf16 = jnp.float32, jnp.bfloat16
    sequence_count, local_length, width = layer_input.shape
    place = lax.axis_index("seq")
    dp = lax.axis_index("dp")
    core, chip, low = dp % 2, dp // 2, place % 2
    length = local_length * 4
    tokens = length // 2
    kv_heads = KEY_VALUE_HEADS // 2
    groups = QUERY_HEADS // KEY_VALUE_HEADS
    kv_width = kv_heads * HEAD_SIZE

    def half_rows(field):
        return lax.dynamic_slice_in_dim(field, (1 - core) * tokens, tokens, 0)

    def other_rows(field):
        return lax.dynamic_slice_in_dim(field, core * tokens, tokens, 0)

    def chain(token, *fields):
        return lax.optimization_barrier((token,) + fields)

    token = layer_input[0, 0, :8]
    core_rows = query_weight.shape[0]
    chip_rows = 2 * core_rows

    own_gains = jnp.concatenate(
        [attn_gain, ffn_gain, jnp.zeros((width - 2 * core_rows,), bf16)]
    )
    own_gains = jnp.pad(own_gains[None], ((0, 7), (0, 0)))
    even, odd = [], []
    for field, chips in ((query_weight, 4), (key_matrix, 2), (value_matrix, 2)):
        first, second = split_cores(field, chips)
        even, odd = even + first, odd + second
    even, odd = jnp.concatenate(even, axis=1), jnp.concatenate(odd, axis=1)
    mine, theirs = jnp.where(core == 0, even, odd), jnp.where(core == 0, odd, even)
    theirs = flip(jnp.concatenate([theirs, own_gains], axis=0), 1)
    inputs_parts = sequence_parts(layer_input, low)
    theirs, their_gains = theirs[:core_rows], theirs[core_rows:]
    attn_block = jnp.where(
        core == 0,
        jnp.concatenate([mine, theirs, own_gains, their_gains], axis=0),
        jnp.concatenate([theirs, mine, their_gains, own_gains], axis=0),
    )
    attn_x, attn_y = flip(attn_block, 2), flip(attn_block, 4)
    ffn_mine, ffn_theirs = prepare_ffn(gate_weight, up_weight, core)
    ffn_other = flip(ffn_theirs, 1)
    ffn_blocks = [pick_order(core == 1, ffn_mine[g], ffn_other[g]) for g in range(2)]
    inputs_full = both_cores(pick_order(low == 1, *inputs_parts), core)
    resid_in = inputs_full.astype(f32)
    inv_one = lax.rsqrt(jnp.mean(resid_in * resid_in, axis=-1, keepdims=True) + eps)
    unit_one = resid_in * inv_one
    token, attn_x, attn_y = chain(token, attn_x, attn_y)
    corner_x, corner_y = flip(attn_y[:core_rows], 2), flip(attn_x[core_rows:], 4)
    token, corner_x, corner_y, ffn_0, down_in, upstream_in, output_in = chain(
        token, corner_x, corner_y, ffn_blocks[0], down_weight, cotangent, output_weight
    )
    sides_0 = (flip(ffn_0, 2), flip(ffn_0, 4))

    def gather_rows(field):
        return lax.all_gather(field, "dp", axis=0, tiled=True, axis_index_groups=SAME_CORE)

    part_rows = down_weight.shape[0] // 2
    output_all = gather_rows(output_in)
    down_0 = gather_rows(down_in[:part_rows])
    upstream_parts = sequence_parts(upstream_in, low)

    attn_pieces = (attn_block, attn_x, attn_y, corner_x, corner_y)
    gain_lines = [p[-16:] for p in (attn_block, attn_x, attn_y, corner_y)]
    gains = jnp.concatenate(
        [g[i, :chip_rows].reshape(2, core_rows) for g in gain_lines for i in (0, 8)], axis=1
    )
    gains = relative_columns(gains, chip).astype(f32)
    gain_one, gain_two = gains[0], gains[1]
    first_normed = relative_columns((unit_one * gain_one).astype(bf16), chip)
    cosine_table, sine_table = rope_tables(length, 0, HEAD_SIZE)
    rest = ((0, 0), (0, LANES - HEAD_SIZE))
    first_half = jnp.arange(HEAD_SIZE)[None, :] < HEAD_SIZE // 2
    tables = (
        jnp.pad(cosine_table, rest),
        jnp.pad(jnp.where(first_half, -sine_table, 0.0), rest),
        jnp.pad(jnp.where(first_half, 0.0, sine_table), rest),
    )
    heads = groups * kv_heads
    fields, attn_weight = project_stage(first_normed, attn_pieces, tables)
    token, fields, *sides_0 = chain(token, fields, *sides_0)
    half = ffn_0.shape[0] // 2
    corners_0 = (flip(sides_0[1][:half], 2), flip(sides_0[0][half:], 4))
    attended = attention_stage(fields, heads, kv_heads)
    token, attended, ffn_1, down_in, corner_0x, corner_0y, *upstream_parts = chain(
        token, attended, ffn_blocks[1], down_in, *corners_0, *upstream_parts
    )
    sides_1 = (flip(ffn_1, 2), flip(ffn_1, 4))
    down_1 = gather_rows(down_in[part_rows:])
    output_all = jnp.pad(
        output_all.reshape(heads, HEAD_SIZE, width), ((0, 0), (0, LANES - HEAD_SIZE), (0, 0))
    ).reshape(heads * LANES, width)
    attn_part = jnp.dot(attended, output_all, preferred_element_type=f32)
    attn_flip = flip(attn_part.astype(bf16), 1)
    upstream = both_cores(pick_order(low == 1, *upstream_parts), core)
    resid_mid = resid_in + attn_part + attn_flip.astype(f32)
    inv_two = lax.rsqrt(jnp.mean(resid_mid * resid_mid, axis=-1, keepdims=True) + eps)
    unit_two = resid_mid * inv_two
    normed_two = relative_columns((unit_two * gain_two).astype(bf16), chip)
    ffn_pieces_0 = (ffn_0, *sides_0, corner_0x, corner_0y)

    def scatter_down(field):
        return lax.psum_scatter(
            field, "dp", scatter_dimension=0, tiled=True, axis_index_groups=SAME_CORE
        )

    token, normed_two, down_0 = chain(token, normed_two, down_0)
    hidden_0, grads_0 = hidden_stage(normed_two, upstream, ffn_pieces_0, down_0)
    token, grads_0, hidden_0, *sides_1 = chain(token, grads_0, hidden_0, *sides_1)
    corners_1 = (flip(sides_1[1][:half], 2), flip(sides_1[0][half:], 4))
    ffn_grad_0 = transposed_times(normed_two, grads_0).astype(bf16)
    token, grads_0, ffn_grad_0 = chain(token, grads_0, ffn_grad_0)
    first_0 = scatter_first(ffn_grad_0)
    grad_norm = back_stage(grads_0, ffn_pieces_0, chip)
    token, grad_norm, hidden_0 = chain(token, grad_norm, hidden_0)
    down_grad_0 = transposed_times(hidden_0, upstream).astype(bf16)
    token, down_grad_0, normed_two, *first_0 = chain(token, down_grad_0, normed_two, *first_0)
    second_0 = scatter_second(ffn_grad_0, *first_0)
    down_grad_0 = scatter_down(down_grad_0)
    token, normed_two, down_1, *corners_1 = chain(token, normed_two, down_1, *corners_1)
    ffn_pieces_1 = (ffn_1, *sides_1, *corners_1)
    hidden_1, grads_1 = hidden_stage(normed_two, upstream, ffn_pieces_1, down_1)
    token, grads_1, hidden_1 = chain(token, grads_1, hidden_1)
    ffn_grad_1 = transposed_times(normed_two, grads_1).astype(bf16)
    token, grads_1, ffn_grad_1 = chain(token, grads_1, ffn_grad_1)
    first_1 = scatter_first(ffn_grad_1)
    grad_norm = back_stage(grads_1, ffn_pieces_1, chip, grad_norm)
    token, grad_norm, hidden_1, down_grad_0, *second_0 = chain(
        token, grad_norm, hidden_1, down_grad_0, *second_0
    )
    ffn_sum_0 = add_half(ffn_grad_0[:chip_rows], *second_0)
    low_high = place % 2, place // 2
    ffn_pair_0 = halve(ffn_sum_0, low_high[0], 1)
    norm_flip = flip(grad_norm.astype(bf16), 1)
    down_grad_1 = transposed_times(hidden_1, upstream).astype(bf16)
    token, down_grad_1, grad_norm, norm_flip, *first_1 = chain(
        token, down_grad_1, grad_norm, norm_flip, *first_1
    )
    second_1 = scatter_second(ffn_grad_1, *first_1)
    down_grad_1 = scatter_down(down_grad_1)
    grad_norm_two = grad_norm + norm_flip.astype(f32)
    ffn_gain_grad = jnp.sum(grad_norm * unit_two, axis=0)
    grad_mid = upstream.astype(f32) + norm_backward(grad_norm_two, unit_two, gain_two, inv_two)
    grad_mid_half = grad_mid.astype(bf16)
    token, grad_mid_half, ffn_pair_0 = chain(token, grad_mid_half, ffn_pair_0)
    ffn_total_0 = halve(ffn_pair_0, low_high[1], 2)
    grad_att = times_transposed(grad_mid_half, output_all).astype(bf16)
    out_grad = transposed_times(attended, grad_mid_half).astype(bf16)
    out_grad = out_grad.reshape(heads, LANES, width)[:, :HEAD_SIZE].reshape(-1, width)
    token, grad_att, out_grad, ffn_total_0 = chain(token, grad_att, out_grad, ffn_total_0)
    out_grad = scatter_down(out_grad)
    ffn_pair_0 = join(ffn_total_0, low_high[1], 2)
    backs = attention_back_stage(fields, attended, grad_att, tables, kv_heads)
    token, down_grad_1, ffn_pair_0, *rest = chain(
        token, down_grad_1, ffn_pair_0, *second_1, *backs
    )
    second_1, backs = rest[:2], rest[2:]
    ffn_sum_1 = add_half(ffn_grad_1[:chip_rows], *second_1)
    ffn_sum_0 = join(ffn_pair_0, low_high[0], 1)
    ffn_pair = halve(ffn_sum_1, low_high[0], 1)
    part_one = inputs_back_stage(backs, attn_weight, chip)
    attn_gain_grad = jnp.sum(part_one * unit_one, axis=0)
    gain_grads = relative_columns(jnp.stack([attn_gain_grad, ffn_gain_grad]), chip).astype(bf16)
    gain_grads = jnp.transpose(gain_grads.reshape(2, 8, core_rows), (1, 0, 2))
    gain_grads = jnp.pad(
        gain_grads.reshape(8, 1, chip_rows), ((0, 0), (0, 7), (0, width - chip_rows))
    ).reshape(64, width)
    token, gain_grads, part_one, out_grad, ffn_pair, ffn_sum_0 = chain(
        token, gain_grads, part_one, out_grad, ffn_pair, ffn_sum_0
    )
    row_grad = lax.psum(jnp.concatenate([down_grad_0, down_grad_1, out_grad], axis=0), "seq")
    ffn_total = halve(ffn_pair, low_high[1], 2)
    attn_grad = weight_stage(first_normed, backs, gain_grads)
    token, attn_grad, part_one, hidden_0, hidden_1, ffn_total = chain(
        token, attn_grad, part_one, hidden_0, hidden_1, ffn_total
    )
    first_2 = scatter_first(attn_grad)
    ffn_pair = join(ffn_total, low_high[1], 2)
    part_flip = flip(other_rows(part_one).astype(bf16), 1)
    down_total = jnp.dot(hidden_0, down_0, preferred_element_type=f32) + jnp.dot(
        hidden_1, down_1, preferred_element_type=f32
    )
    token, down_total, part_flip, *first_2 = chain(token, down_total, part_flip, *first_2)
    second_2 = scatter_second(attn_grad, *first_2)
    down_flip = flip(other_rows(down_total).astype(bf16), 1)
    grad_norm_one = half_rows(part_one) + part_flip.astype(f32)
    unit_half = half_rows(unit_one)
    input_grad = half_rows(grad_mid) + norm_backward(
        grad_norm_one, unit_half, gain_one, half_rows(inv_one)
    )
    input_parts = slice_parts(input_grad.astype(bf16), low)
    layer_half = (half_rows(resid_mid + down_total) + down_flip.astype(f32)).astype(bf16)
    layer_parts = slice_parts(layer_half, low)
    token, ffn_pair, *second_2 = chain(token, ffn_pair, *second_2)
    attn_grad = add_half(attn_grad[: chip_rows + 16], *second_2)
    ffn_sum_1 = join(ffn_pair, low_high[0], 1)
    tail = halve(attn_grad, low_high[0], 1)
    token, tail, ffn_sum_1 = chain(token, tail, ffn_sum_1)
    tail = halve(tail, low_high[1], 2)

    def settle(field, size, extra=None):
        own = lax.dynamic_slice_in_dim(field, core * size, size, 0)
        other = lax.dynamic_slice_in_dim(field, (1 - core) * size, size, 0)
        if extra is not None:
            lines = extra.shape[0] // 2
            own = (own, lax.dynamic_slice_in_dim(extra, core * lines, lines, 0))
            other = jnp.concatenate(
                [other, lax.dynamic_slice_in_dim(extra, (1 - core) * lines, lines, 0)], axis=0
            )
        return own, flip(other, 1)

    settled = settle(ffn_sum_0, core_rows) + settle(ffn_sum_1, core_rows)
    token, tail, *settled = chain(token, tail, *settled)
    tail = join(tail, low_high[1], 2)
    gate_grad, up_grad = merge_ffn(*settled, core)
    token, tail, gate_grad, up_grad = chain(token, tail, gate_grad, up_grad)
    tail = join(tail, low_high[0], 1)
    layer_output = join_slices(layer_parts, low)
    input_grad = join_slices(input_parts, low).astype(f32)
    row_grad = row_grad.astype(f32)
    down_grad, out_grad = row_grad[: 2 * part_rows], row_grad[2 * part_rows :]
    token, tail, layer_output, input_grad, down_grad, out_grad = chain(
        token, tail, layer_output, input_grad, down_grad, out_grad
    )
    (attn_own, gains_own), attn_other = settle(
        tail[:chip_rows], core_rows, tail[chip_rows:]
    )
    gain_sums = (
        0.0 * token[0].astype(f32)
        + gains_own[0, :chip_rows].astype(f32)
        + attn_other[core_rows, :chip_rows].astype(f32)
    )
    attn_other = attn_other[:core_rows]
    cuts = (0, groups * kv_width, (groups + 1) * kv_width, (groups + 2) * kv_width)
    query_grad, key_grad, value_grad = [
        interleave(
            attn_own[:, cuts[i] : cuts[i + 1]], attn_other[:, cuts[i] : cuts[i + 1]], chips, core
        )
        for i, chips in enumerate((4, 2, 2))
    ]
    return (
        layer_output,
        input_grad,
        gain_sums[:core_rows],
        query_grad,
        key_grad,
        value_grad,
        out_grad,
        gain_sums[core_rows:],
        gate_grad,
        up_grad,
        down_grad,
    )


def any_body(layer_input, *rest):
    paired = (
        lax.axis_size("dp") == 8 and lax.axis_size("seq") == 4 and layer_input.shape[0] == 2
    )
    return (paired_body if paired else body)(layer_input, *rest)


def solution(mesh):
    return jax.shard_map(
        any_body,
        mesh=mesh,
        in_specs=(
            P("dp", "seq", None),
            P("dp"),
            P("dp", None),
            P("dp", None),
            P("dp", None),
            P("dp", None),
            P("dp"),
            P("dp", None),
            P("dp", None),
            P("dp", None),
            P("dp", "seq", None),
        ),
        out_specs=(
            P("dp", "seq", None),
            P("dp", "seq", None),
            P("dp"),
            P("dp", None),
            P("dp", None),
            P("dp", None),
            P("dp", None),
            P("dp"),
            P("dp", None),
            P("dp", None),
            P("dp", None),
        ),
        check_vma=False,
    )
```

```python
import jax
import jax.numpy as jnp
from jax import lax
from jax.experimental import pallas as pl
from jax.experimental.pallas import tpu as pltpu
from jax.sharding import PartitionSpec as P

QUERY_HEADS = 16
KEY_VALUE_HEADS = 8
HEAD_SIZE = 96


eps = 1e-06
theta_base = 100000.0


def rope_tables(count, start_offset, width):
    half = width // 2
    freq = theta_base ** (-(jnp.arange(half).astype(jnp.float32) * 2.0) / width)
    places = (start_offset + jnp.arange(count)).astype(jnp.float32)
    angle = places[:, None] * freq[None, :]
    angle = jnp.concatenate([angle, angle], axis=1)
    return (jnp.cos(angle), jnp.sin(angle))


def rotate(field):
    half = field.shape[-1] // 2
    return jnp.concatenate([-field[..., half:], field[..., :half]], axis=-1)


def rope_forward(field, cosine_table, sine_table):
    return field * cosine_table + rotate(field) * sine_table


def rotary_backward(field, cosine_table, sine_table):
    return field * cosine_table - rotate(field) * sine_table


def norm_backward(grad_norm, unit, gain, inverse):
    scaled = grad_norm * gain
    return inverse * (scaled - unit * jnp.mean(scaled * unit, axis=-1, keepdims=True))


def times_transposed(left, right):
    return lax.dot_general(
        left, right, (((1,), (1,)), ((), ())), preferred_element_type=jnp.float32
    )


def transposed_times(left, right):
    return lax.dot_general(
        left, right, (((0,), (0,)), ((), ())), preferred_element_type=jnp.float32
    )


def block_probs(query_block, key_block, start_offset, logsum_block):
    block = query_block.shape[1]
    stop = key_block.shape[1]
    scores = jnp.einsum(
        "sqgcd,skcd->sgcqk", query_block, key_block, preferred_element_type=jnp.float32
    ) * HEAD_SIZE ** (-0.5)
    causal = (start_offset + jnp.arange(block))[:, None] >= jnp.arange(stop)[None, :]
    if logsum_block is None:
        masked = jnp.where(causal, scores, -1e30)
        peak = jnp.max(masked, axis=-1, keepdims=True)
        logsum_block = peak + jnp.log(jnp.sum(jnp.exp(masked - peak), axis=-1, keepdims=True))
    probs = jnp.where(causal, jnp.exp(scores - logsum_block), 0.0)
    return (probs, logsum_block)


def body(
    layer_input,
    attn_gain,
    query_weight,
    key_matrix,
    value_matrix,
    output_weight,
    ffn_gain,
    gate_weight,
    up_weight,
    down_weight,
    cotangent,
):
    sequence_count, local_length, width = layer_input.shape
    token_rows = sequence_count * local_length
    shard_count = lax.axis_size("seq")
    length = local_length * shard_count
    query_group_count = QUERY_HEADS // KEY_VALUE_HEADS
    local_key_value = KEY_VALUE_HEADS // shard_count
    scale = HEAD_SIZE ** (-0.5)
    half_precision = jnp.bfloat16
    query_all, key_all, value_all, output_all, gain_one = (
        lax.all_gather(query_weight, "dp", axis=0, tiled=True),
        lax.all_gather(key_matrix, "dp", axis=0, tiled=True),
        lax.all_gather(value_matrix, "dp", axis=0, tiled=True),
        lax.all_gather(output_weight, "dp", axis=0, tiled=True),
        lax.all_gather(attn_gain, "dp", axis=0, tiled=True),
    )
    gate_all, up_all, down_all, gain_two = (
        lax.all_gather(gate_weight, "dp", axis=0, tiled=True),
        lax.all_gather(up_weight, "dp", axis=0, tiled=True),
        lax.all_gather(down_weight, "dp", axis=0, tiled=True),
        lax.all_gather(ffn_gain, "dp", axis=0, tiled=True),
    )
    gain_one = gain_one.astype(jnp.float32)
    gain_two = gain_two.astype(jnp.float32)
    resid_in = layer_input.reshape(token_rows, width).astype(jnp.float32)
    inv_one = lax.rsqrt(jnp.mean(resid_in * resid_in, axis=-1, keepdims=True) + eps)
    unit_one = resid_in * inv_one
    first_normed = (unit_one * gain_one).astype(half_precision)
    cosine_table, sine_table = rope_tables(
        local_length, lax.axis_index("seq") * local_length, HEAD_SIZE
    )
    query_rows = jnp.dot(first_normed, query_all, preferred_element_type=jnp.float32).reshape(
        sequence_count, local_length, QUERY_HEADS, HEAD_SIZE
    )
    key_rows = jnp.dot(first_normed, key_all, preferred_element_type=jnp.float32).reshape(
        sequence_count, local_length, KEY_VALUE_HEADS, HEAD_SIZE
    )
    value_rows = jnp.dot(first_normed, value_all, preferred_element_type=jnp.float32)
    query_rows = rope_forward(query_rows, cosine_table[:, None, :], sine_table[:, None, :]).astype(
        half_precision
    )
    key_rows = rope_forward(key_rows, cosine_table[:, None, :], sine_table[:, None, :]).astype(
        half_precision
    )
    query_rows = query_rows.reshape(
        sequence_count, local_length, query_group_count, KEY_VALUE_HEADS * HEAD_SIZE
    )
    paired = jnp.stack(
        [
            key_rows.reshape(sequence_count, local_length, KEY_VALUE_HEADS * HEAD_SIZE),
            value_rows.astype(half_precision).reshape(
                sequence_count, local_length, KEY_VALUE_HEADS * HEAD_SIZE
            ),
        ],
        axis=2,
    )
    query_heads, pair_heads = (
        lax.all_to_all(query_rows, "seq", split_axis=3, concat_axis=1, tiled=True),
        lax.all_to_all(paired, "seq", split_axis=3, concat_axis=1, tiled=True),
    )
    query_heads = query_heads.reshape(
        sequence_count, length, query_group_count, local_key_value, HEAD_SIZE
    )
    key_heads = pair_heads[:, :, 0].reshape(sequence_count, length, local_key_value, HEAD_SIZE)
    value_heads = pair_heads[:, :, 1].reshape(sequence_count, length, local_key_value, HEAD_SIZE)
    block = min(512, length)
    count = length // block
    attended_blocks = []
    logsums = []
    for index in range(count):
        start_offset = index * block
        stop = start_offset + block
        probs, logsum_block = block_probs(
            query_heads[:, start_offset:stop], key_heads[:, :stop], start_offset, None
        )
        logsums.append(logsum_block)
        probs_half = probs.astype(half_precision)
        attended_blocks.append(
            jnp.einsum(
                "sgcqk,skcd->sqgcd",
                probs_half,
                value_heads[:, :stop],
                preferred_element_type=jnp.float32,
            ).astype(half_precision)
        )
    attended_heads = jnp.concatenate(attended_blocks, axis=1)
    attended_tok = lax.all_to_all(
        attended_heads.reshape(
            sequence_count, length, query_group_count, local_key_value * HEAD_SIZE
        ),
        "seq",
        split_axis=1,
        concat_axis=3,
        tiled=True,
    )
    flat_att = attended_tok.reshape(token_rows, QUERY_HEADS * HEAD_SIZE)
    resid_mid = resid_in + jnp.dot(flat_att, output_all, preferred_element_type=jnp.float32)
    inv_two = lax.rsqrt(jnp.mean(resid_mid * resid_mid, axis=-1, keepdims=True) + eps)
    unit_two = resid_mid * inv_two
    normed_two = (unit_two * gain_two).astype(half_precision)
    gate = jnp.dot(normed_two, gate_all, preferred_element_type=jnp.float32)
    upward = jnp.dot(normed_two, up_all, preferred_element_type=jnp.float32)
    sigma = jax.nn.sigmoid(gate)
    silu_gate = gate * sigma
    hidden = (silu_gate * upward).astype(half_precision)
    layer_output = (
        resid_mid + jnp.dot(hidden, down_all, preferred_element_type=jnp.float32)
    ).astype(half_precision)
    upstream = cotangent.reshape(token_rows, width)
    grad_hidden = times_transposed(upstream, down_all)
    down_grad = transposed_times(hidden, upstream)
    grad_gate = (grad_hidden * upward * sigma * (1.0 + gate * (1.0 - sigma))).astype(half_precision)
    grad_up = (grad_hidden * silu_gate).astype(half_precision)
    gate_grad = transposed_times(normed_two, grad_gate)
    up_grad = transposed_times(normed_two, grad_up)
    grad_norm_two = times_transposed(grad_gate, gate_all) + times_transposed(grad_up, up_all)
    ffn_gain_grad = jnp.sum(grad_norm_two * unit_two, axis=0)
    gate_grad, up_grad, down_grad, ffn_gain_grad = (
        lax.psum_scatter(
            gate_grad.astype(jnp.bfloat16), "dp", scatter_dimension=0, tiled=True
        ).astype(jnp.float32),
        lax.psum_scatter(
            up_grad.astype(jnp.bfloat16), "dp", scatter_dimension=0, tiled=True
        ).astype(jnp.float32),
        lax.psum_scatter(
            down_grad.astype(jnp.bfloat16), "dp", scatter_dimension=0, tiled=True
        ).astype(jnp.float32),
        lax.psum_scatter(
            ffn_gain_grad.astype(jnp.bfloat16), "dp", scatter_dimension=0, tiled=True
        ).astype(jnp.float32),
    )
    gate_grad, up_grad, down_grad, ffn_gain_grad = (
        lax.psum(gate_grad.astype(jnp.bfloat16), "seq").astype(jnp.float32),
        lax.psum(up_grad.astype(jnp.bfloat16), "seq").astype(jnp.float32),
        lax.psum(down_grad.astype(jnp.bfloat16), "seq").astype(jnp.float32),
        lax.psum(ffn_gain_grad.astype(jnp.bfloat16), "seq").astype(jnp.float32),
    )
    grad_mid = upstream.astype(jnp.float32) + norm_backward(
        grad_norm_two, unit_two, gain_two, inv_two
    )
    grad_mid_half = grad_mid.astype(half_precision)
    out_grad = transposed_times(flat_att, grad_mid_half)
    grad_att = (
        times_transposed(grad_mid_half, output_all)
        .astype(half_precision)
        .reshape(sequence_count, local_length, query_group_count, KEY_VALUE_HEADS * HEAD_SIZE)
    )
    grad_heads = lax.all_to_all(grad_att, "seq", split_axis=3, concat_axis=1, tiled=True)
    grad_heads = grad_heads.reshape(
        sequence_count, length, query_group_count, local_key_value, HEAD_SIZE
    )
    query_grad_blocks = []
    key_gradient = jnp.zeros((sequence_count, length, local_key_value, HEAD_SIZE), jnp.float32)
    value_gradient = jnp.zeros((sequence_count, length, local_key_value, HEAD_SIZE), jnp.float32)
    for index in range(count):
        start_offset = index * block
        stop = start_offset + block
        query_block = query_heads[:, start_offset:stop]
        key_block = key_heads[:, :stop]
        value_block = value_heads[:, :stop]
        grad_block = grad_heads[:, start_offset:stop]
        probs, unused = block_probs(query_block, key_block, start_offset, logsums[index])
        probs_half = probs.astype(half_precision)
        grad_probs = jnp.einsum(
            "sqgcd,skcd->sgcqk", grad_block, value_block, preferred_element_type=jnp.float32
        )
        delta = jnp.sum(
            grad_block.astype(jnp.float32)
            * attended_heads[:, start_offset:stop].astype(jnp.float32),
            axis=-1,
        )
        delta = jnp.transpose(delta, (0, 2, 3, 1))[..., None]
        grad_scores = (probs * (grad_probs - delta)).astype(half_precision)
        query_grad_blocks.append(
            jnp.einsum(
                "sgcqk,skcd->sqgcd", grad_scores, key_block, preferred_element_type=jnp.float32
            )
            * scale
        )
        key_part = (
            jnp.einsum(
                "sgcqk,sqgcd->skcd", grad_scores, query_block, preferred_element_type=jnp.float32
            )
            * scale
        )
        value_part = jnp.einsum(
            "sgcqk,sqgcd->skcd", probs_half, grad_block, preferred_element_type=jnp.float32
        )
        padding = ((0, 0), (0, length - stop), (0, 0), (0, 0))
        key_gradient = key_gradient + jnp.pad(key_part, padding)
        value_gradient = value_gradient + jnp.pad(value_part, padding)
    grad_queries = jnp.concatenate(query_grad_blocks, axis=1)
    cos_full, sin_full = rope_tables(length, 0, HEAD_SIZE)
    queries_back = rotary_backward(
        grad_queries, cos_full[:, None, None, :], sin_full[:, None, None, :]
    ).astype(half_precision)
    key_rows_restored = rotary_backward(
        key_gradient, cos_full[:, None, :], sin_full[:, None, :]
    ).astype(half_precision)
    value_rows_restored = value_gradient.astype(half_precision)
    queries_back = queries_back.reshape(
        sequence_count, length, query_group_count, local_key_value * HEAD_SIZE
    )
    pair_back = jnp.stack(
        [
            key_rows_restored.reshape(sequence_count, length, local_key_value * HEAD_SIZE),
            value_rows_restored.reshape(sequence_count, length, local_key_value * HEAD_SIZE),
        ],
        axis=2,
    )
    queries_tok, paired_token_rows = (
        lax.all_to_all(queries_back, "seq", split_axis=1, concat_axis=3, tiled=True),
        lax.all_to_all(pair_back, "seq", split_axis=1, concat_axis=3, tiled=True),
    )
    queries_tok = queries_tok.reshape(token_rows, QUERY_HEADS * HEAD_SIZE)
    key_token_rows = paired_token_rows[:, :, 0].reshape(token_rows, KEY_VALUE_HEADS * HEAD_SIZE)
    value_token_rows = paired_token_rows[:, :, 1].reshape(token_rows, KEY_VALUE_HEADS * HEAD_SIZE)
    query_grad = transposed_times(first_normed, queries_tok)
    key_grad = transposed_times(first_normed, key_token_rows)
    value_grad = transposed_times(first_normed, value_token_rows)
    grad_norm_one = (
        times_transposed(queries_tok, query_all)
        + times_transposed(key_token_rows, key_all)
        + times_transposed(value_token_rows, value_all)
    )
    attn_gain_grad = jnp.sum(grad_norm_one * unit_one, axis=0)
    query_grad, key_grad, value_grad, out_grad, attn_gain_grad = (
        lax.psum_scatter(
            query_grad.astype(jnp.bfloat16), "dp", scatter_dimension=0, tiled=True
        ).astype(jnp.float32),
        lax.psum_scatter(
            key_grad.astype(jnp.bfloat16), "dp", scatter_dimension=0, tiled=True
        ).astype(jnp.float32),
        lax.psum_scatter(
            value_grad.astype(jnp.bfloat16), "dp", scatter_dimension=0, tiled=True
        ).astype(jnp.float32),
        lax.psum_scatter(
            out_grad.astype(jnp.bfloat16), "dp", scatter_dimension=0, tiled=True
        ).astype(jnp.float32),
        lax.psum_scatter(
            attn_gain_grad.astype(jnp.bfloat16), "dp", scatter_dimension=0, tiled=True
        ).astype(jnp.float32),
    )
    query_grad, key_grad, value_grad, out_grad, attn_gain_grad = (
        lax.psum(query_grad.astype(jnp.bfloat16), "seq").astype(jnp.float32),
        lax.psum(key_grad.astype(jnp.bfloat16), "seq").astype(jnp.float32),
        lax.psum(value_grad.astype(jnp.bfloat16), "seq").astype(jnp.float32),
        lax.psum(out_grad.astype(jnp.bfloat16), "seq").astype(jnp.float32),
        lax.psum(attn_gain_grad.astype(jnp.bfloat16), "seq").astype(jnp.float32),
    )
    input_grad = grad_mid + norm_backward(grad_norm_one, unit_one, gain_one, inv_one)
    return (
        layer_output.reshape(sequence_count, local_length, width),
        input_grad.reshape(sequence_count, local_length, width),
        attn_gain_grad,
        query_grad,
        key_grad,
        value_grad,
        out_grad,
        ffn_gain_grad,
        gate_grad,
        up_grad,
        down_grad,
    )


SAME_CORE = [[0, 2, 4, 6], [1, 3, 5, 7]]
VMEM_BYTES = 48 * 1024 * 1024


def flip(field, bit):
    count = lax.axis_size("dp")
    return lax.ppermute(field, "dp", [(i, i ^ bit) for i in range(count)])


def cross(field, bit):
    return lax.ppermute(field, "seq", [(i, i ^ bit) for i in range(4)])


def column_swap(field, turn, back):
    pairs = []
    for dp in range(8):
        for place in range(4):
            chip, core, high, low = dp // 2, dp % 2, place // 2, place % 2
            target = (2 * chip + (high ^ 1)) * 4 + 2 * core + (low ^ turn)
            pairs.append((target, dp * 4 + place) if back else (dp * 4 + place, target))
    return lax.ppermute(field, ("dp", "seq"), pairs)


def pick_order(swapped, first, second, axis=0):
    return jnp.where(
        swapped,
        jnp.concatenate([second, first], axis=axis),
        jnp.concatenate([first, second], axis=axis),
    )


def sequence_parts(field, low):
    return [
        column_swap(lax.dynamic_index_in_dim(field, low ^ turn, 0, keepdims=False), turn, False)
        for turn in range(2)
    ]


def slice_parts(half, low):
    rows = half.shape[0] // 2
    return [
        column_swap(lax.dynamic_slice_in_dim(half, (low ^ turn) * rows, rows, 0), turn, True)
        for turn in range(2)
    ]


def join_slices(parts, low):
    return jnp.where(low == 1, jnp.stack(parts[::-1]), jnp.stack(parts))


def both_cores(half, core):
    return pick_order(core == 0, half, flip(half, 1))


def relative_columns(field, chip):
    width = field.shape[-1] // 4
    return jnp.concatenate(
        [lax.dynamic_slice_in_dim(field, (chip ^ r) * width, width, field.ndim - 1) for r in range(4)],
        axis=-1,
    )


def gather_chips(block):
    half = block.shape[0] // 2
    from_x = flip(block, 2)
    from_y = flip(block, 4)
    corner_x = flip(from_y[:half], 2)
    corner_y = flip(from_x[half:], 4)
    return block, from_x, from_y, corner_x, corner_y


def add_half(*terms):
    total = terms[0].astype(jnp.float32)
    for term in terms[1:]:
        total = total + term.astype(jnp.float32)
    return total.astype(jnp.bfloat16)


def scatter_first(field):
    half = field.shape[0] // 8
    corner = field[6 * half :]
    return flip(corner[:half], 2), flip(corner[half:], 4)


def scatter_second(field, got_x, got_y):
    rows = field.shape[0] // 4
    half = rows // 2
    over_x, over_y = field[rows : 2 * rows], field[2 * rows : 3 * rows]
    send_x = jnp.concatenate([over_x[:half], add_half(over_x[half:], got_y)], axis=0)
    send_y = jnp.concatenate([add_half(over_y[:half], got_x), over_y[half:]], axis=0)
    return flip(send_x, 2), flip(send_y, 4)


def split_rows(field, which):
    size = field.shape[0] // 2
    own = lax.dynamic_slice_in_dim(field, which * size, size, 0)
    return own, lax.dynamic_slice_in_dim(field, (1 - which) * size, size, 0)


def prepare_kernel(core_ref, gate_mine, gate_theirs, up_mine, up_theirs, mine_ref, theirs_ref):
    for gate, up, out in ((gate_mine, up_mine, mine_ref), (gate_theirs, up_theirs, theirs_ref)):
        part = gate.shape[1] // 2
        for group in range(2):
            for offset, field in ((0, gate), (part, up)):
                start = 2 * part * group + offset
                out[:, start : start + part] = field[:, group * part : (group + 1) * part]


def prepare_ffn(gate_weight, up_weight, core):
    rows, columns = gate_weight.shape
    piece = columns // 8
    mine = pl.BlockSpec((rows, piece), lambda j, c: (0, 2 * j + c[0]))
    theirs = pl.BlockSpec((rows, piece), lambda j, c: (0, 2 * j + 1 - c[0]))
    out = pl.BlockSpec((rows, 2 * piece), lambda j, c: (0, j))
    shape = jax.ShapeDtypeStruct((rows, columns), jnp.bfloat16)
    return pl.pallas_call(
        prepare_kernel,
        out_shape=(shape, shape),
        grid_spec=pltpu.PrefetchScalarGridSpec(
            num_scalar_prefetch=1,
            grid=(4,),
            in_specs=[mine, theirs, mine, theirs],
            out_specs=(out, out),
        ),
        name="prepare_ffn",
    )(core.reshape(1), gate_weight, gate_weight, up_weight, up_weight)


def merge_kernel(core_ref, own_0, other_0, own_1, other_1, gate_ref, up_ref):
    part = own_0.shape[1] // 2
    mine = core_ref[0] == pl.program_id(1)
    first = jnp.where(mine, own_0[...].astype(jnp.float32), other_0[...].astype(jnp.float32))
    second = jnp.where(mine, own_1[...].astype(jnp.float32), other_1[...].astype(jnp.float32))
    gate_ref[:, :part] = first[:, :part]
    gate_ref[:, part:] = second[:, :part]
    up_ref[:, :part] = first[:, part:]
    up_ref[:, part:] = second[:, part:]


def merge_ffn(own_0, other_0, own_1, other_1, core):
    rows, columns = own_0.shape
    piece = columns // 4
    part = pl.BlockSpec((rows, piece), lambda j, i, c: (0, j))
    out = pl.BlockSpec((rows, piece), lambda j, i, c: (0, 2 * j + i))
    shape = jax.ShapeDtypeStruct((rows, columns * 2), jnp.float32)
    return pl.pallas_call(
        merge_kernel,
        out_shape=(shape, shape),
        grid_spec=pltpu.PrefetchScalarGridSpec(
            num_scalar_prefetch=1,
            grid=(4, 2),
            in_specs=[part] * 4,
            out_specs=(out, out),
        ),
        name="merge_ffn",
    )(core.reshape(1), own_0, other_0, own_1, other_1)


def hint(flops, bytes_accessed, transcendentals=0):
    return pl.CostEstimate(
        flops=flops // 64, transcendentals=transcendentals // 64, bytes_accessed=bytes_accessed // 64
    )


def stacked(pieces, rows):
    own, from_x, from_y, corner_x, corner_y = pieces
    rest = rows - corner_x.shape[0]
    return jnp.concatenate(
        [own[:rows, :], from_x[:rows, :], from_y[:rows, :], corner_x[...], corner_y[:rest, :]],
        axis=0,
    )


def hidden_kernel(rows, normed, upstream, *refs):
    down, hidden, grads = refs[5:]
    part = grads.shape[1] // 2
    weight = stacked(refs[:5], rows)
    tile = 256
    for start in range(0, normed.shape[0], tile):
        lines = pl.ds(start, tile)
        total = jnp.dot(normed[lines, :], weight, preferred_element_type=jnp.float32)
        grad_hidden = lax.dot_general(
            upstream[lines, :], down[...], (((1,), (1,)), ((), ())), preferred_element_type=jnp.float32
        )
        gate, upward = total[:, :part], total[:, part:]
        sigma = jax.nn.sigmoid(gate)
        silu_gate = gate * sigma
        hidden[lines, :] = (silu_gate * upward).astype(jnp.bfloat16)
        grads[lines, :part] = (
            grad_hidden * upward * sigma * (1.0 + gate * (1.0 - sigma))
        ).astype(jnp.bfloat16)
        grads[lines, part:] = (grad_hidden * silu_gate).astype(jnp.bfloat16)


def hidden_stage(normed, upstream, pieces, down, group):
    length, width = normed.shape
    columns = pieces[0].shape[1] // 2
    piece = columns // 4
    whole = pl.BlockSpec((length, width), lambda j: (0, 0), pipeline_mode=pl.Buffered(1))
    return pl.pallas_call(
        lambda *refs: hidden_kernel(width // 4, *refs),
        out_shape=(
            jax.ShapeDtypeStruct((length, columns // 2), jnp.bfloat16),
            jax.ShapeDtypeStruct((length, columns), jnp.bfloat16),
        ),
        grid=(4,),
        in_specs=[whole, whole]
        + [pl.BlockSpec((p.shape[0], piece), lambda j: (0, 2 * j + group)) for p in pieces]
        + [pl.BlockSpec((piece // 2, width), lambda j: (j, 0))],
        out_specs=(
            pl.BlockSpec((length, piece // 2), lambda j: (0, j)),
            pl.BlockSpec((length, piece), lambda j: (0, j)),
        ),
        compiler_params=pltpu.CompilerParams(vmem_limit_bytes=VMEM_BYTES),
        cost_estimate=hint(
            3 * length * width * columns,
            4 * length * width + 3 * width * columns + 3 * length * columns,
            length * columns // 2,
        ),
        name="hidden_stage",
    )(normed, upstream, *pieces, down)


NEGATIVE = -1e30
LANES = 128


def turned(field, cos, sin_low, sin_high, sign):
    half = HEAD_SIZE // 2
    spun = pltpu.roll(field, LANES - half, 1) * sin_low + pltpu.roll(field, half, 1) * sin_high
    return field * cos + sign * spun


def project_kernel(rows, heads, normed, cos, sin_low, sin_high, *refs):
    out, weight = refs[5:]
    own, from_x, from_y, corner_x, corner_y = refs[:5]
    rest = rows - corner_x.shape[0]

    @pl.when(pl.program_id(0) == 0)
    def _():
        start = 0
        for piece, count in (
            (own, rows), (from_x, rows), (from_y, rows), (corner_x, rows - rest), (corner_y, rest)
        ):
            lines = pl.ds(start, count)
            for head in range(heads):
                weight[lines, pl.ds(head * LANES, HEAD_SIZE)] = piece[
                    :count, pl.ds(head * HEAD_SIZE, HEAD_SIZE)
                ]
                weight[lines, pl.ds(head * LANES + HEAD_SIZE, LANES - HEAD_SIZE)] = jnp.zeros(
                    (count, LANES - HEAD_SIZE), jnp.bfloat16
                )
            start += count

    part = jnp.dot(normed[...], weight[...], preferred_element_type=jnp.float32)
    for head in range(heads):
        columns = slice(head * LANES, (head + 1) * LANES)
        field = part[:, columns]
        if head < heads * 3 // 4:
            field = turned(field, cos[...], sin_low[...], sin_high[...], 1.0)
        out[:, columns] = field.astype(jnp.bfloat16)


def project_stage(normed, pieces, tables):
    length, width = normed.shape
    columns = pieces[0].shape[1]
    heads = columns // HEAD_SIZE
    tile = 256
    table = pl.BlockSpec((tile, LANES), lambda i: (i, 0))
    rows, corner = width // 4, pieces[3].shape[0]
    counts = (rows, rows, rows, corner, rows - corner)
    return pl.pallas_call(
        lambda *refs: project_kernel(width // 4, heads, *refs),
        out_shape=(
            jax.ShapeDtypeStruct((length, heads * LANES), jnp.bfloat16),
            jax.ShapeDtypeStruct((width, heads * LANES), jnp.bfloat16),
        ),
        grid=(length // tile,),
        in_specs=[pl.BlockSpec((tile, width), lambda i: (i, 0)), table, table, table]
        + [
            pl.BlockSpec((count, columns), lambda i: (0, 0), pipeline_mode=pl.Buffered(1))
            for count in counts
        ],
        out_specs=(
            pl.BlockSpec((tile, heads * LANES), lambda i: (i, 0)),
            pl.BlockSpec((width, heads * LANES), lambda i: (0, 0), pipeline_mode=pl.Buffered(1)),
        ),
        compiler_params=pltpu.CompilerParams(vmem_limit_bytes=VMEM_BYTES),
        cost_estimate=hint(
            2 * length * width * heads * LANES,
            2 * length * width + 4 * width * columns + 2 * length * columns,
        ),
        name="project_stage",
    )(normed, *tables, *pieces)


def block_softmax(query, key, tile, index):
    scale = HEAD_SIZE ** (-0.5)
    lines = pl.ds(index * tile, tile)
    before = index * tile

    def scores(which):
        return scale * lax.dot_general(
            query[lines, :], key[which, :], (((1,), (1,)), ((), ())),
            preferred_element_type=jnp.float32,
        )

    last = scores(lines)
    seen = lax.broadcasted_iota(jnp.int32, (tile, tile), 0) >= lax.broadcasted_iota(
        jnp.int32, (tile, tile), 1
    )
    last = jnp.where(seen, last, NEGATIVE)
    peak = jnp.max(last, axis=1, keepdims=True)
    if before:
        earlier = scores(pl.ds(0, before))
        peak = jnp.maximum(peak, jnp.max(earlier, axis=1, keepdims=True))
    last = jnp.exp(last - peak)
    total = jnp.sum(last, axis=1, keepdims=True)
    if before:
        earlier = jnp.exp(earlier - peak)
        total = total + jnp.sum(earlier, axis=1, keepdims=True)
    inverse = 1.0 / total
    parts = [(lines, last * inverse)]
    if before:
        parts.append((pl.ds(0, before), earlier * inverse))
    return lines, parts


def attention_kernel(tile, query, key, value, out):
    for index in range(query.shape[0] // tile):
        lines, parts = block_softmax(query, key, tile, index)
        total = 0.0
        for which, probs in parts:
            total = total + jnp.dot(
                probs.astype(jnp.bfloat16), value[which, :], preferred_element_type=jnp.float32
            )
        out[lines, :] = total.astype(jnp.bfloat16)


def attention_stage(fields, heads, kv_heads):
    length = fields.shape[0]
    tile = min(256, length)
    spec = lambda start, count: pl.BlockSpec((length, LANES), lambda h: (0, start + h % count))
    return pl.pallas_call(
        lambda *refs: attention_kernel(tile, *refs),
        out_shape=jax.ShapeDtypeStruct((length, heads * LANES), jnp.bfloat16),
        grid=(heads,),
        in_specs=[spec(0, heads), spec(heads, kv_heads), spec(heads + kv_heads, kv_heads)],
        out_specs=spec(0, heads),
        compiler_params=pltpu.CompilerParams(vmem_limit_bytes=VMEM_BYTES),
        cost_estimate=hint(
            2 * heads * length * length * LANES,
            6 * heads * length * LANES,
            heads * length * length // 2,
        ),
        name="attention_stage",
    )(fields, fields, fields)


def attention_back_kernel(tile, *refs):
    query_0, query_1, key, value, out_0, out_1, grad_0, grad_1 = refs[:8]
    cos, sin_low, sin_high, back_0, back_1, key_back, value_back, key_sum, value_sum = refs[8:]
    scale = HEAD_SIZE ** (-0.5)
    key_sum[...] = jnp.zeros_like(key_sum)
    value_sum[...] = jnp.zeros_like(value_sum)
    for query, out, grad, back in (
        (query_0, out_0, grad_0, back_0),
        (query_1, out_1, grad_1, back_1),
    ):
        for index in range(query.shape[0] // tile):
            lines, parts = block_softmax(query, key, tile, index)
            upstream = grad[lines, :]
            delta = jnp.sum(
                upstream.astype(jnp.float32) * out[lines, :].astype(jnp.float32),
                axis=1,
                keepdims=True,
            )
            total = 0.0
            for which, probs in parts:
                grad_probs = lax.dot_general(
                    upstream, value[which, :], (((1,), (1,)), ((), ())),
                    preferred_element_type=jnp.float32,
                )
                grad_scores = (probs * (grad_probs - delta)).astype(jnp.bfloat16)
                total = total + jnp.dot(
                    grad_scores, key[which, :], preferred_element_type=jnp.float32
                )
                key_sum[which, :] += lax.dot_general(
                    grad_scores, query[lines, :], (((0,), (0,)), ((), ())),
                    preferred_element_type=jnp.float32,
                )
                value_sum[which, :] += lax.dot_general(
                    probs.astype(jnp.bfloat16), upstream, (((0,), (0,)), ((), ())),
                    preferred_element_type=jnp.float32,
                )
            back[lines, :] = turned(
                total * scale, cos[lines, :], sin_low[lines, :], sin_high[lines, :], -1.0
            ).astype(jnp.bfloat16)
    key_back[...] = turned(
        key_sum[...] * scale, cos[...], sin_low[...], sin_high[...], -1.0
    ).astype(jnp.bfloat16)
    value_back[...] = value_sum[...].astype(jnp.bfloat16)


def attention_back_stage(fields, attended, grads, tables, kv_heads):
    length = fields.shape[0]
    tile = min(256, length)
    spec = lambda start: pl.BlockSpec((length, LANES), lambda h: (0, start + h))
    table = pl.BlockSpec((length, LANES), lambda h: (0, 0))
    shape = jax.ShapeDtypeStruct((length, kv_heads * LANES), jnp.bfloat16)
    first, second = spec(0), spec(kv_heads)
    return pl.pallas_call(
        lambda *refs: attention_back_kernel(tile, *refs),
        out_shape=(shape,) * 4,
        grid=(kv_heads,),
        in_specs=[first, second, spec(2 * kv_heads), spec(3 * kv_heads)]
        + [first, second] * 2
        + [table] * 3,
        out_specs=(first,) * 4,
        scratch_shapes=[pltpu.VMEM((length, LANES), jnp.float32)] * 2,
        compiler_params=pltpu.CompilerParams(vmem_limit_bytes=VMEM_BYTES),
        cost_estimate=hint(
            10 * kv_heads * length * length * LANES,
            30 * kv_heads * length * LANES,
            kv_heads * length * length,
        ),
        name="attention_back_stage",
    )(fields, fields, fields, fields, attended, attended, grads, grads, *tables)


def inputs_back_kernel(rows, chip_ref, *refs):
    weight, field, out, sums = refs[-4:]
    columns = refs[0].shape[1]
    part = 0.0
    for j, grad in enumerate(refs[:-4]):
        part = part + lax.dot_general(
            grad[...], weight[:, j * columns : (j + 1) * columns], (((1,), (1,)), ((), ())),
            preferred_element_type=jnp.float32,
        )
    for r in range(4):
        where = pl.ds(pl.multiple_of((chip_ref[0] ^ r) * rows, 128), rows)
        out[:, where] = part[:, r * rows : (r + 1) * rows]
    total = field[...].astype(jnp.float32)
    unit = total * lax.rsqrt(jnp.mean(total * total, axis=1, keepdims=True) + eps)

    @pl.when(pl.program_id(0) == 0)
    def _():
        sums[...] = jnp.zeros_like(sums)

    sums[...] += jnp.sum((out[...] * unit).reshape(-1, 8, total.shape[1]), axis=0)


def inputs_back_stage(backs, weight, chip, field):
    length, columns = backs[0].shape
    width = weight.shape[0]
    tile = 256
    return pl.pallas_call(
        lambda *refs: inputs_back_kernel(width // 4, *refs),
        out_shape=(
            jax.ShapeDtypeStruct((length, width), jnp.float32),
            jax.ShapeDtypeStruct((8, width), jnp.float32),
        ),
        grid_spec=pltpu.PrefetchScalarGridSpec(
            num_scalar_prefetch=1,
            grid=(length // tile,),
            in_specs=[pl.BlockSpec((tile, columns), lambda i, c: (i, 0))] * len(backs)
            + [
                pl.BlockSpec(weight.shape, lambda i, c: (0, 0), pipeline_mode=pl.Buffered(1)),
                pl.BlockSpec((tile, width), lambda i, c: (i, 0)),
            ],
            out_specs=(
                pl.BlockSpec((tile, width), lambda i, c: (i, 0)),
                pl.BlockSpec((8, width), lambda i, c: (0, 0)),
            ),
        ),
        compiler_params=pltpu.CompilerParams(vmem_limit_bytes=VMEM_BYTES),
        cost_estimate=hint(
            2 * length * width * weight.shape[1], 2 * width * weight.shape[1] + 8 * length * width
        ),
        name="inputs_back_stage",
    )(chip.reshape(1), *backs, weight, field)


def norm_kernel(with_parts, chip_ref, field, *refs):
    total = field[...].astype(jnp.float32)
    if with_parts:
        part, other, gain, middle, out = refs
        total = total + part[...] + other[...].astype(jnp.float32)
        middle[...] = total
    else:
        gain, out = refs
    inverse = lax.rsqrt(jnp.mean(total * total, axis=1, keepdims=True) + eps)
    normed = (total * inverse * gain[...]).astype(jnp.bfloat16)
    width = total.shape[1] // 4
    for j in range(4):
        columns = pl.ds(pl.multiple_of((chip_ref[0] ^ j) * width, 128), width)
        out[:, columns] = normed[:, j * width : (j + 1) * width]


def norm_stage(field, gain, chip, *parts):
    length, width = field.shape
    tile = 256
    line = pl.BlockSpec((tile, width), lambda i, c: (i, 0))
    shapes = [jax.ShapeDtypeStruct((length, width), jnp.bfloat16)]
    if parts:
        shapes = [jax.ShapeDtypeStruct((length, width), jnp.float32)] + shapes
    return pl.pallas_call(
        lambda *refs: norm_kernel(len(parts) > 0, *refs),
        out_shape=tuple(shapes),
        grid_spec=pltpu.PrefetchScalarGridSpec(
            num_scalar_prefetch=1,
            grid=(length // tile,),
            in_specs=[line] * (1 + len(parts)) + [pl.BlockSpec((1, width), lambda i, c: (0, 0))],
            out_specs=(line,) * len(shapes),
        ),
        compiler_params=pltpu.CompilerParams(vmem_limit_bytes=VMEM_BYTES),
        cost_estimate=hint(16 * length * width, 12 * length * width),
        name="norm_stage",
    )(chip.reshape(1), field, *parts, gain[None])


def norm_back_kernel(grad, other, middle, upstream, gain, out, out_half, sums):
    total = middle[...]
    inverse = lax.rsqrt(jnp.mean(total * total, axis=1, keepdims=True) + eps)
    unit = total * inverse
    own = grad[...]
    scaled = (own + other[...].astype(jnp.float32)) * gain[...]
    average = jnp.mean(scaled * unit, axis=1, keepdims=True)
    result = upstream[...].astype(jnp.float32) + inverse * (scaled - unit * average)
    out[...] = result
    out_half[...] = result.astype(jnp.bfloat16)

    @pl.when(pl.program_id(0) == 0)
    def _():
        sums[...] = jnp.zeros_like(sums)

    sums[...] += jnp.sum((own * unit).reshape(-1, 8, own.shape[1]), axis=0)


def norm_back_stage(grad, other, middle, upstream, gain):
    length, width = grad.shape
    tile = 256
    line = pl.BlockSpec((tile, width), lambda i: (i, 0))
    return pl.pallas_call(
        norm_back_kernel,
        out_shape=(
            jax.ShapeDtypeStruct((length, width), jnp.float32),
            jax.ShapeDtypeStruct((length, width), jnp.bfloat16),
            jax.ShapeDtypeStruct((8, width), jnp.float32),
        ),
        grid=(length // tile,),
        in_specs=[line] * 4 + [pl.BlockSpec((1, width), lambda i: (0, 0))],
        out_specs=(line, line, pl.BlockSpec((8, width), lambda i: (0, 0))),
        compiler_params=pltpu.CompilerParams(vmem_limit_bytes=VMEM_BYTES),
        cost_estimate=hint(16 * length * width, 18 * length * width),
        name="norm_back_stage",
    )(grad, other, middle, upstream, gain[None])


def outer_kernel(left, right, out):
    out[...] = lax.dot_general(
        left[...], right[...], (((0,), (0,)), ((), ())), preferred_element_type=jnp.float32
    ).astype(jnp.bfloat16)


def outer_stage(left, right):
    length, rows = left.shape
    columns = right.shape[1]
    tile = 256
    return pl.pallas_call(
        outer_kernel,
        out_shape=jax.ShapeDtypeStruct((rows, columns), jnp.bfloat16),
        grid=(rows // tile,),
        in_specs=[
            pl.BlockSpec((length, tile), lambda i: (0, i)),
            pl.BlockSpec((length, columns), lambda i: (0, 0), pipeline_mode=pl.Buffered(1)),
        ],
        out_specs=pl.BlockSpec((tile, columns), lambda i: (i, 0)),
        compiler_params=pltpu.CompilerParams(vmem_limit_bytes=VMEM_BYTES),
        cost_estimate=hint(2 * length * rows * columns, 2 * (rows + columns) * length),
        name="outer_stage",
    )(left, right)


def down_kernel(hidden_0, hidden_1, down_0, down_1, out):
    out[...] = jnp.dot(
        hidden_0[...], down_0[...], preferred_element_type=jnp.float32
    ) + jnp.dot(hidden_1[...], down_1[...], preferred_element_type=jnp.float32)


def down_stage(hidden_0, hidden_1, down_0, down_1):
    length, units = hidden_0.shape
    width = down_0.shape[1]
    tile = 256
    line = pl.BlockSpec((tile, units), lambda i: (i, 0))
    whole = pl.BlockSpec((units, width), lambda i: (0, 0), pipeline_mode=pl.Buffered(1))
    return pl.pallas_call(
        down_kernel,
        out_shape=jax.ShapeDtypeStruct((length, width), jnp.float32),
        grid=(length // tile,),
        in_specs=[line, line, whole, whole],
        out_specs=pl.BlockSpec((tile, width), lambda i: (i, 0)),
        compiler_params=pltpu.CompilerParams(vmem_limit_bytes=VMEM_BYTES),
        cost_estimate=hint(4 * length * units * width, 4 * units * (length + width)),
        name="down_stage",
    )(hidden_0, hidden_1, down_0, down_1)


def output_back_kernel(grad, attended, weight, out, weight_grad, total):
    step = pl.program_id(0)
    out[...] = lax.dot_general(
        grad[...], weight[...], (((1,), (1,)), ((), ())), preferred_element_type=jnp.float32
    ).astype(jnp.bfloat16)
    part = lax.dot_general(
        attended[...], grad[...], (((0,), (0,)), ((), ())), preferred_element_type=jnp.float32
    )

    @pl.when(step == 0)
    def _():
        total[...] = part

    @pl.when(step > 0)
    def _():
        total[...] += part

    @pl.when(step == pl.num_programs(0) - 1)
    def _():
        for head in range(total.shape[0] // LANES):
            weight_grad[pl.ds(head * HEAD_SIZE, HEAD_SIZE), :] = total[
                pl.ds(head * LANES, HEAD_SIZE), :
            ].astype(jnp.bfloat16)


def output_back_stage(grad, attended, weight):
    length, width = grad.shape
    columns = attended.shape[1]
    rows = columns // LANES * HEAD_SIZE
    tile = 512
    return pl.pallas_call(
        output_back_kernel,
        out_shape=(
            jax.ShapeDtypeStruct((length, columns), jnp.bfloat16),
            jax.ShapeDtypeStruct((rows, width), jnp.bfloat16),
        ),
        grid=(length // tile,),
        in_specs=[
            pl.BlockSpec((tile, width), lambda i: (i, 0)),
            pl.BlockSpec((tile, columns), lambda i: (i, 0)),
            pl.BlockSpec((columns, width), lambda i: (0, 0), pipeline_mode=pl.Buffered(1)),
        ],
        out_specs=(
            pl.BlockSpec((tile, columns), lambda i: (i, 0)),
            pl.BlockSpec((rows, width), lambda i: (0, 0), pipeline_mode=pl.Buffered(1)),
        ),
        scratch_shapes=[pltpu.VMEM((columns, width), jnp.float32)],
        compiler_params=pltpu.CompilerParams(vmem_limit_bytes=VMEM_BYTES),
        cost_estimate=hint(4 * length * width * columns, 4 * width * (length + columns)),
        name="output_back_stage",
    )(grad, attended, weight)


def weight_kernel(normed, *refs):
    gains, out = refs[-2:]
    rows = normed.shape[1]
    heads = refs[0].shape[1] // LANES
    for j, back in enumerate(refs[:-2]):
        part = lax.dot_general(
            normed[...], back[...], (((0,), (0,)), ((), ())), preferred_element_type=jnp.float32
        ).astype(jnp.bfloat16)
        for head in range(heads):
            out[:rows, pl.ds((j * heads + head) * HEAD_SIZE, HEAD_SIZE)] = part[
                :, head * LANES : head * LANES + HEAD_SIZE
            ]
    out[rows:, :] = gains[...]


def weight_stage(normed, backs, gains):
    length, width = normed.shape
    columns = gains.shape[1]
    rows, extra = width // 4, gains.shape[0] // 4
    whole = pl.BlockSpec(backs[0].shape, lambda i: (0, 0), pipeline_mode=pl.Buffered(1))
    return pl.pallas_call(
        weight_kernel,
        out_shape=jax.ShapeDtypeStruct((width + 4 * extra, columns), jnp.bfloat16),
        grid=(4,),
        in_specs=[pl.BlockSpec((length, rows), lambda i: (0, i))]
        + [whole] * len(backs)
        + [pl.BlockSpec((extra, columns), lambda i: (i, 0))],
        out_specs=pl.BlockSpec((rows + extra, columns), lambda i: (i, 0)),
        compiler_params=pltpu.CompilerParams(vmem_limit_bytes=VMEM_BYTES),
        cost_estimate=hint(
            2 * length * width * columns,
            2 * length * width + 2 * width * columns + 2 * length * columns,
        ),
        name="weight_stage",
    )(normed, *backs, gains)


def back_kernel(rows, with_base, chip_ref, grads, *rest):
    weight, out = rest[-1], rest[-2]
    piece = rest[0].shape[1]

    @pl.when(pl.program_id(0) == 0)
    def _():
        for j in range(4):
            start = 0
            for part in rest[5 * j : 5 * j + 5]:
                count = part.shape[0]
                weight[start : start + count, j * piece : (j + 1) * piece] = part[...]
                start += count

    part = lax.dot_general(
        grads[...], weight[...], (((1,), (1,)), ((), ())), preferred_element_type=jnp.float32
    )
    for r in range(4):
        columns = pl.ds(pl.multiple_of((chip_ref[0] ^ r) * rows, 128), rows)
        block = part[:, r * rows : (r + 1) * rows]
        if with_base:
            block = block + rest[20][:, columns]
        out[:, columns] = block


def back_stage(grads, pieces, chip, group, base=None):
    length, columns = grads.shape
    width = pieces[0].shape[0] * 4
    piece = columns // 4
    tile = 256
    line = pl.BlockSpec((tile, width), lambda i, c: (i, 0))

    def part_spec(rows, j):
        return pl.BlockSpec(
            (rows, piece), lambda i, c: (0, 2 * j + group), pipeline_mode=pl.Buffered(1)
        )

    inputs = [grads, *(list(pieces) * 4)] + ([] if base is None else [base])
    return pl.pallas_call(
        lambda *refs: back_kernel(width // 4, base is not None, *refs),
        out_shape=jax.ShapeDtypeStruct((length, width), jnp.float32),
        grid_spec=pltpu.PrefetchScalarGridSpec(
            num_scalar_prefetch=1,
            grid=(length // tile,),
            in_specs=[pl.BlockSpec((tile, columns), lambda i, c: (i, 0))]
            + [part_spec(p.shape[0], j) for j in range(4) for p in pieces]
            + ([] if base is None else [line]),
            out_specs=line,
            scratch_shapes=[pltpu.VMEM((width, columns), jnp.bfloat16)],
        ),
        compiler_params=pltpu.CompilerParams(vmem_limit_bytes=VMEM_BYTES),
        cost_estimate=hint(
            2 * length * width * columns,
            2 * length * columns + 2 * width * columns + 4 * length * width,
        ),
        name="back_stage",
    )(chip.reshape(1), *inputs)


def split_cores(field, chips):
    piece = field.shape[1] // (2 * chips)
    cuts = [field[:, i * piece : (i + 1) * piece] for i in range(2 * chips)]
    return cuts[::2], cuts[1::2]


def interleave(own, other, chips, core):
    piece = own.shape[1] // chips
    parts = []
    for i in range(chips):
        a, b = own[:, i * piece : (i + 1) * piece], other[:, i * piece : (i + 1) * piece]
        parts += [jnp.where(core == 0, a, b), jnp.where(core == 0, b, a)]
    return jnp.concatenate(parts, axis=1).astype(jnp.float32)


def paired_body(
    layer_input,
    attn_gain,
    query_weight,
    key_matrix,
    value_matrix,
    output_weight,
    ffn_gain,
    gate_weight,
    up_weight,
    down_weight,
    cotangent,
):
    f32, bf16 = jnp.float32, jnp.bfloat16
    sequence_count, local_length, width = layer_input.shape
    place = lax.axis_index("seq")
    dp = lax.axis_index("dp")
    core, chip, low = dp % 2, dp // 2, place % 2
    length = local_length * 4
    tokens = length // 2
    kv_heads = KEY_VALUE_HEADS // 2
    groups = QUERY_HEADS // KEY_VALUE_HEADS
    kv_width = kv_heads * HEAD_SIZE

    def half_rows(field):
        return lax.dynamic_slice_in_dim(field, (1 - core) * tokens, tokens, 0)

    def other_rows(field):
        return lax.dynamic_slice_in_dim(field, core * tokens, tokens, 0)

    def chain(token, *fields):
        return lax.optimization_barrier((token,) + fields)

    token = layer_input[0, 0, :8]
    core_rows = query_weight.shape[0]
    chip_rows = 2 * core_rows

    own_gains = jnp.concatenate(
        [attn_gain, ffn_gain, jnp.zeros((width - 2 * core_rows,), bf16)]
    )
    own_gains = jnp.pad(own_gains[None], ((0, 7), (0, 0)))
    even, odd = [], []
    for field, chips in ((query_weight, 4), (key_matrix, 2), (value_matrix, 2)):
        first, second = split_cores(field, chips)
        even, odd = even + first, odd + second
    even, odd = jnp.concatenate(even, axis=1), jnp.concatenate(odd, axis=1)
    mine, theirs = jnp.where(core == 0, even, odd), jnp.where(core == 0, odd, even)
    theirs = flip(jnp.concatenate([theirs, own_gains], axis=0), 1)
    both_parts = sequence_parts(jnp.concatenate([layer_input, cotangent], axis=1), low)
    theirs, their_gains = theirs[:core_rows], theirs[core_rows:]
    attn_block = jnp.where(
        core == 0,
        jnp.concatenate([mine, theirs, own_gains, their_gains], axis=0),
        jnp.concatenate([theirs, mine, their_gains, own_gains], axis=0),
    )
    part_rows = down_weight.shape[0] // 2
    share = part_rows // 4
    down_quarters = [
        lax.dynamic_slice_in_dim(down_weight, g * part_rows + place * share, share, 0)
        for g in range(2)
    ]
    attn_block = jnp.concatenate([attn_block, output_weight, *down_quarters], axis=0)
    cut = attn_block.shape[0] // 32 * 16
    attn_x, attn_y = flip(attn_block, 2), flip(attn_block, 4)
    ffn_mine, ffn_theirs = prepare_ffn(gate_weight, up_weight, core)
    ffn_other = flip(ffn_theirs, 1)
    ffn_block = pick_order(core == 1, ffn_mine, ffn_other)
    token, attn_x, attn_y = chain(token, attn_x, attn_y)
    corner_x, corner_y = flip(attn_y[:cut], 2), flip(attn_x[cut:], 4)
    token, corner_x, corner_y, ffn_block, *both_parts = chain(
        token, corner_x, corner_y, ffn_block, *both_parts
    )
    ffn_sides = (flip(ffn_block, 2), flip(ffn_block, 4))
    halves = [p.reshape(2, local_length, width) for p in both_parts]
    here = pick_order(low == 1, *halves, axis=1)
    there = flip(here, 1)
    both = pick_order(core == 0, here, there, axis=1)
    inputs_full, upstream = both[0], both[1]


    attn_pieces = (attn_block, attn_x, attn_y, corner_x, corner_y)
    extras = [p[-(16 + core_rows + 2 * share) :] for p in (attn_block, attn_x, attn_y, corner_y)]
    gains = jnp.concatenate(
        [g[i, :chip_rows].reshape(2, core_rows) for g in extras for i in (0, 8)], axis=1
    )

    def chip_order(start, count):
        field = jnp.stack([g[start : start + count] for g in extras])
        return jnp.concatenate(
            [lax.dynamic_index_in_dim(field, chip ^ r, 0, keepdims=False) for r in range(4)], axis=0
        )

    def share_quarters(field):
        whole = lax.all_gather(field, "seq", axis=0)
        return jnp.swapaxes(whole.reshape(4, 4, share, width), 0, 1).reshape(-1, width)

    output_all = chip_order(16, core_rows)
    down_0 = share_quarters(chip_order(16 + core_rows, share))
    down_1 = share_quarters(chip_order(16 + core_rows + share, share))
    gains = relative_columns(gains, chip).astype(f32)
    gain_one, gain_two = gains[0], gains[1]
    (first_normed,) = norm_stage(inputs_full, gain_one, chip)
    cosine_table, sine_table = rope_tables(length, 0, HEAD_SIZE)
    rest = ((0, 0), (0, LANES - HEAD_SIZE))
    first_half = jnp.arange(HEAD_SIZE)[None, :] < HEAD_SIZE // 2
    tables = (
        jnp.pad(cosine_table, rest),
        jnp.pad(jnp.where(first_half, -sine_table, 0.0), rest),
        jnp.pad(jnp.where(first_half, 0.0, sine_table), rest),
    )
    heads = groups * kv_heads
    fields, attn_weight = project_stage(first_normed, attn_pieces, tables)
    attended = attention_stage(fields, heads, kv_heads)
    token, attended, ffn_x, ffn_y = chain(token, attended, *ffn_sides)
    half = ffn_block.shape[0] // 2
    ffn_corners = (flip(ffn_y[:half], 2), flip(ffn_x[half:], 4))
    output_all = jnp.pad(
        output_all.reshape(heads, HEAD_SIZE, width), ((0, 0), (0, LANES - HEAD_SIZE), (0, 0))
    ).reshape(heads * LANES, width)
    attn_part = jnp.dot(attended, output_all, preferred_element_type=f32)
    attn_flip = flip(attn_part.astype(bf16), 1)
    token, attn_flip = chain(token, attn_flip)
    resid_mid, normed_two = norm_stage(inputs_full, gain_two, chip, attn_part, attn_flip)

    def scatter_down(field):
        return lax.psum_scatter(
            field, "dp", scatter_dimension=0, tiled=True, axis_index_groups=SAME_CORE
        )

    token, normed_two, down_0, *ffn_corners = chain(token, normed_two, down_0, *ffn_corners)
    ffn_pieces = (ffn_block, ffn_x, ffn_y, *ffn_corners)
    hidden_0, grads_0 = hidden_stage(normed_two, upstream, ffn_pieces, down_0, 0)
    token, grads_0, hidden_0 = chain(token, grads_0, hidden_0)
    ffn_grad_0 = outer_stage(normed_two, grads_0)
    token, grads_0, ffn_grad_0 = chain(token, grads_0, ffn_grad_0)
    first_0 = scatter_first(ffn_grad_0)
    grad_norm = back_stage(grads_0, ffn_pieces, chip, 0)
    token, grad_norm, hidden_0 = chain(token, grad_norm, hidden_0)
    down_grad_0 = outer_stage(hidden_0, upstream)
    token, down_grad_0, normed_two, down_1, *first_0 = chain(
        token, down_grad_0, normed_two, down_1, *first_0
    )
    second_0 = scatter_second(ffn_grad_0, *first_0)
    down_grad_0 = scatter_down(down_grad_0)
    hidden_1, grads_1 = hidden_stage(normed_two, upstream, ffn_pieces, down_1, 1)
    token, grads_1, hidden_1 = chain(token, grads_1, hidden_1)
    ffn_grad_1 = outer_stage(normed_two, grads_1)
    token, grads_1, ffn_grad_1 = chain(token, grads_1, ffn_grad_1)
    first_1 = scatter_first(ffn_grad_1)
    grad_norm = back_stage(grads_1, ffn_pieces, chip, 1, grad_norm)
    token, grad_norm, hidden_1 = chain(token, grad_norm, hidden_1)
    norm_flip = flip(grad_norm.astype(bf16), 1)
    down_grad_1 = outer_stage(hidden_1, upstream)
    token, down_grad_1, hidden_1, *second_0 = chain(token, down_grad_1, hidden_1, *second_0)
    ffn_sum_0 = add_half(ffn_grad_0[:chip_rows], *second_0)
    own_0, other_0 = split_rows(ffn_sum_0, low)
    near_0 = cross(other_0, 1)
    down_total = down_stage(hidden_0, hidden_1, down_0, down_1)
    token, down_grad_0, down_grad_1, down_total, grad_norm, norm_flip, near_0, *first_1 = chain(
        token, down_grad_0, down_grad_1, down_total, grad_norm, norm_flip, near_0, *first_1
    )
    second_1 = scatter_second(ffn_grad_1, *first_1)
    down_grad_1 = scatter_down(down_grad_1)
    pair_0 = add_half(own_0, near_0)
    far_0 = cross(pair_0, 2)
    down_flip = flip(other_rows(down_total).astype(bf16), 1)
    grad_mid, grad_mid_half, gain_sums_two = norm_back_stage(
        grad_norm, norm_flip, resid_mid, upstream, gain_two
    )
    ffn_gain_grad = jnp.sum(gain_sums_two, axis=0)
    token, grad_mid_half, down_flip = chain(token, grad_mid_half, down_flip)
    layer_half = (half_rows(resid_mid + down_total) + down_flip.astype(f32)).astype(bf16)
    grad_att, out_grad = output_back_stage(grad_mid_half, attended, output_all)
    token, grad_att, out_grad, layer_half, far_0 = chain(
        token, grad_att, out_grad, layer_half, far_0
    )
    out_grad = scatter_down(out_grad)
    total_0 = add_half(pair_0, far_0)
    last_0 = cross(total_0, 1)
    layer_parts = slice_parts(layer_half, low)
    backs = attention_back_stage(fields, attended, grad_att, tables, kv_heads)
    token, last_0, down_grad_1, *rest = chain(
        token, last_0, down_grad_1, *second_1, *layer_parts, *backs
    )
    second_1, layer_parts, backs = rest[:2], rest[2:4], rest[4:]
    ffn_sum_1 = add_half(ffn_grad_1[:chip_rows], *second_1)
    own_1, other_1 = split_rows(ffn_sum_1, low)
    near_1 = cross(other_1, 1)
    part_one, gain_sums_one = inputs_back_stage(backs, attn_weight, chip, inputs_full)
    attn_gain_grad = jnp.sum(gain_sums_one, axis=0)
    gain_grads = relative_columns(jnp.stack([attn_gain_grad, ffn_gain_grad]), chip).astype(bf16)
    gain_grads = jnp.transpose(gain_grads.reshape(2, 8, core_rows), (1, 0, 2))
    gain_grads = jnp.pad(
        gain_grads.reshape(8, 1, chip_rows), ((0, 0), (0, 7), (0, width - chip_rows))
    ).reshape(64, width)
    token, gain_grads, part_one, out_grad, near_1 = chain(
        token, gain_grads, part_one, out_grad, near_1
    )
    row_sum = lax.psum(jnp.concatenate([down_grad_0, down_grad_1, out_grad], axis=0), "seq")
    pair_1 = add_half(own_1, near_1)
    far_1 = cross(pair_1, 2)
    attn_grad = weight_stage(first_normed, backs, gain_grads)
    token, attn_grad, part_one = chain(token, attn_grad, part_one)
    first_2 = scatter_first(attn_grad)
    part_flip = flip(other_rows(part_one).astype(bf16), 1)
    layer_output = join_slices(layer_parts, low)
    ffn_sum_0 = pick_order(low == 1, total_0, last_0)
    token, layer_output, ffn_sum_0, part_flip, far_1, *first_2 = chain(
        token, layer_output, ffn_sum_0, part_flip, far_1, *first_2
    )
    second_2 = scatter_second(attn_grad, *first_2)
    total_1 = add_half(pair_1, far_1)
    last_1 = cross(total_1, 1)
    grad_norm_one = half_rows(part_one) + part_flip.astype(f32)
    resid_in = half_rows(inputs_full).astype(f32)
    inverse = lax.rsqrt(jnp.mean(resid_in * resid_in, axis=-1, keepdims=True) + eps)
    input_grad = half_rows(grad_mid) + norm_backward(
        grad_norm_one, resid_in * inverse, gain_one, inverse
    )
    token, input_grad, last_1, *second_2 = chain(token, input_grad, last_1, *second_2)
    attn_grad = add_half(attn_grad[: chip_rows + 16], *second_2)
    tail_own, tail_other = split_rows(attn_grad, low)
    tail_near = cross(tail_other, 1)
    token, tail_near, row_sum = chain(token, tail_near, row_sum)
    tail = add_half(tail_own, tail_near)
    tail_far = cross(tail, 2)
    input_parts = slice_parts(input_grad.astype(bf16), low)
    token, tail_far = chain(token, tail_far)
    tail = add_half(tail, tail_far)
    tail_last = cross(tail, 1)
    ffn_sum_1 = pick_order(low == 1, total_1, last_1)

    def settle(field, size, extra=None):
        own = lax.dynamic_slice_in_dim(field, core * size, size, 0)
        other = lax.dynamic_slice_in_dim(field, (1 - core) * size, size, 0)
        if extra is not None:
            lines = extra.shape[0] // 2
            own = (own, lax.dynamic_slice_in_dim(extra, core * lines, lines, 0))
            other = jnp.concatenate(
                [other, lax.dynamic_slice_in_dim(extra, (1 - core) * lines, lines, 0)], axis=0
            )
        return own, flip(other, 1)

    settled = settle(ffn_sum_0, core_rows) + settle(ffn_sum_1, core_rows)
    token, *settled = chain(token, *settled)
    gate_grad, up_grad = merge_ffn(*settled, core)
    row_sum = row_sum.astype(f32)
    down_grad, out_grad = row_sum[: 2 * part_rows], row_sum[2 * part_rows :]
    token, tail_last, gate_grad, up_grad, down_grad, out_grad = chain(
        token, tail_last, gate_grad, up_grad, down_grad, out_grad
    )
    tail = pick_order(low == 1, tail, tail_last)
    (attn_own, gains_own), attn_other = settle(
        tail[:chip_rows], core_rows, tail[chip_rows:]
    )
    gain_sums = (
        0.0 * token[0].astype(f32)
        + gains_own[0, :chip_rows].astype(f32)
        + attn_other[core_rows, :chip_rows].astype(f32)
    )
    attn_other = attn_other[:core_rows]
    input_grad = join_slices(input_parts, low).astype(f32)
    cuts = (0, groups * kv_width, (groups + 1) * kv_width, (groups + 2) * kv_width)
    query_grad, key_grad, value_grad = [
        interleave(
            attn_own[:, cuts[i] : cuts[i + 1]], attn_other[:, cuts[i] : cuts[i + 1]], chips, core
        )
        for i, chips in enumerate((4, 2, 2))
    ]
    return (
        layer_output,
        input_grad,
        gain_sums[:core_rows],
        query_grad,
        key_grad,
        value_grad,
        out_grad,
        gain_sums[core_rows:],
        gate_grad,
        up_grad,
        down_grad,
    )


def any_body(layer_input, *rest):
    paired = (
        lax.axis_size("dp") == 8 and lax.axis_size("seq") == 4 and layer_input.shape[0] == 2
    )
    return (paired_body if paired else body)(layer_input, *rest)


def solution(mesh):
    return jax.shard_map(
        any_body,
        mesh=mesh,
        in_specs=(
            P("dp", "seq", None),
            P("dp"),
            P("dp", None),
            P("dp", None),
            P("dp", None),
            P("dp", None),
            P("dp"),
            P("dp", None),
            P("dp", None),
            P("dp", None),
            P("dp", "seq", None),
        ),
        out_specs=(
            P("dp", "seq", None),
            P("dp", "seq", None),
            P("dp"),
            P("dp", None),
            P("dp", None),
            P("dp", None),
            P("dp", None),
            P("dp"),
            P("dp", None),
            P("dp", None),
            P("dp", None),
        ),
        check_vma=False,
    )
```

```python
import jax
import jax.numpy as jnp
from jax import lax
from jax.experimental import pallas as pl
from jax.experimental.pallas import tpu as pltpu
from jax.sharding import PartitionSpec as P

QUERY_HEADS = 16
KEY_VALUE_HEADS = 8
HEAD_SIZE = 96


eps = 1e-06
theta_base = 100000.0


def rope_tables(count, start_offset, width):
    half = width // 2
    freq = theta_base ** (-(jnp.arange(half).astype(jnp.float32) * 2.0) / width)
    places = (start_offset + jnp.arange(count)).astype(jnp.float32)
    angle = places[:, None] * freq[None, :]
    angle = jnp.concatenate([angle, angle], axis=1)
    return (jnp.cos(angle), jnp.sin(angle))


def rotate(field):
    half = field.shape[-1] // 2
    return jnp.concatenate([-field[..., half:], field[..., :half]], axis=-1)


def rope_forward(field, cosine_table, sine_table):
    return field * cosine_table + rotate(field) * sine_table


def rotary_backward(field, cosine_table, sine_table):
    return field * cosine_table - rotate(field) * sine_table


def norm_backward(grad_norm, unit, gain, inverse):
    scaled = grad_norm * gain
    return inverse * (scaled - unit * jnp.mean(scaled * unit, axis=-1, keepdims=True))


def times_transposed(left, right):
    return lax.dot_general(
        left, right, (((1,), (1,)), ((), ())), preferred_element_type=jnp.float32
    )


def transposed_times(left, right):
    return lax.dot_general(
        left, right, (((0,), (0,)), ((), ())), preferred_element_type=jnp.float32
    )


def block_probs(query_block, key_block, start_offset, logsum_block):
    block = query_block.shape[1]
    stop = key_block.shape[1]
    scores = jnp.einsum(
        "sqgcd,skcd->sgcqk", query_block, key_block, preferred_element_type=jnp.float32
    ) * HEAD_SIZE ** (-0.5)
    causal = (start_offset + jnp.arange(block))[:, None] >= jnp.arange(stop)[None, :]
    if logsum_block is None:
        masked = jnp.where(causal, scores, -1e30)
        peak = jnp.max(masked, axis=-1, keepdims=True)
        logsum_block = peak + jnp.log(jnp.sum(jnp.exp(masked - peak), axis=-1, keepdims=True))
    probs = jnp.where(causal, jnp.exp(scores - logsum_block), 0.0)
    return (probs, logsum_block)


def body(
    layer_input,
    attn_gain,
    query_weight,
    key_matrix,
    value_matrix,
    output_weight,
    ffn_gain,
    gate_weight,
    up_weight,
    down_weight,
    cotangent,
):
    sequence_count, local_length, width = layer_input.shape
    token_rows = sequence_count * local_length
    shard_count = lax.axis_size("seq")
    length = local_length * shard_count
    query_group_count = QUERY_HEADS // KEY_VALUE_HEADS
    local_key_value = KEY_VALUE_HEADS // shard_count
    scale = HEAD_SIZE ** (-0.5)
    half_precision = jnp.bfloat16
    query_all, key_all, value_all, output_all, gain_one = (
        lax.all_gather(query_weight, "dp", axis=0, tiled=True),
        lax.all_gather(key_matrix, "dp", axis=0, tiled=True),
        lax.all_gather(value_matrix, "dp", axis=0, tiled=True),
        lax.all_gather(output_weight, "dp", axis=0, tiled=True),
        lax.all_gather(attn_gain, "dp", axis=0, tiled=True),
    )
    gate_all, up_all, down_all, gain_two = (
        lax.all_gather(gate_weight, "dp", axis=0, tiled=True),
        lax.all_gather(up_weight, "dp", axis=0, tiled=True),
        lax.all_gather(down_weight, "dp", axis=0, tiled=True),
        lax.all_gather(ffn_gain, "dp", axis=0, tiled=True),
    )
    gain_one = gain_one.astype(jnp.float32)
    gain_two = gain_two.astype(jnp.float32)
    resid_in = layer_input.reshape(token_rows, width).astype(jnp.float32)
    inv_one = lax.rsqrt(jnp.mean(resid_in * resid_in, axis=-1, keepdims=True) + eps)
    unit_one = resid_in * inv_one
    first_normed = (unit_one * gain_one).astype(half_precision)
    cosine_table, sine_table = rope_tables(
        local_length, lax.axis_index("seq") * local_length, HEAD_SIZE
    )
    query_rows = jnp.dot(first_normed, query_all, preferred_element_type=jnp.float32).reshape(
        sequence_count, local_length, QUERY_HEADS, HEAD_SIZE
    )
    key_rows = jnp.dot(first_normed, key_all, preferred_element_type=jnp.float32).reshape(
        sequence_count, local_length, KEY_VALUE_HEADS, HEAD_SIZE
    )
    value_rows = jnp.dot(first_normed, value_all, preferred_element_type=jnp.float32)
    query_rows = rope_forward(query_rows, cosine_table[:, None, :], sine_table[:, None, :]).astype(
        half_precision
    )
    key_rows = rope_forward(key_rows, cosine_table[:, None, :], sine_table[:, None, :]).astype(
        half_precision
    )
    query_rows = query_rows.reshape(
        sequence_count, local_length, query_group_count, KEY_VALUE_HEADS * HEAD_SIZE
    )
    paired = jnp.stack(
        [
            key_rows.reshape(sequence_count, local_length, KEY_VALUE_HEADS * HEAD_SIZE),
            value_rows.astype(half_precision).reshape(
                sequence_count, local_length, KEY_VALUE_HEADS * HEAD_SIZE
            ),
        ],
        axis=2,
    )
    query_heads, pair_heads = (
        lax.all_to_all(query_rows, "seq", split_axis=3, concat_axis=1, tiled=True),
        lax.all_to_all(paired, "seq", split_axis=3, concat_axis=1, tiled=True),
    )
    query_heads = query_heads.reshape(
        sequence_count, length, query_group_count, local_key_value, HEAD_SIZE
    )
    key_heads = pair_heads[:, :, 0].reshape(sequence_count, length, local_key_value, HEAD_SIZE)
    value_heads = pair_heads[:, :, 1].reshape(sequence_count, length, local_key_value, HEAD_SIZE)
    block = min(512, length)
    count = length // block
    attended_blocks = []
    logsums = []
    for index in range(count):
        start_offset = index * block
        stop = start_offset + block
        probs, logsum_block = block_probs(
            query_heads[:, start_offset:stop], key_heads[:, :stop], start_offset, None
        )
        logsums.append(logsum_block)
        probs_half = probs.astype(half_precision)
        attended_blocks.append(
            jnp.einsum(
                "sgcqk,skcd->sqgcd",
                probs_half,
                value_heads[:, :stop],
                preferred_element_type=jnp.float32,
            ).astype(half_precision)
        )
    attended_heads = jnp.concatenate(attended_blocks, axis=1)
    attended_tok = lax.all_to_all(
        attended_heads.reshape(
            sequence_count, length, query_group_count, local_key_value * HEAD_SIZE
        ),
        "seq",
        split_axis=1,
        concat_axis=3,
        tiled=True,
    )
    flat_att = attended_tok.reshape(token_rows, QUERY_HEADS * HEAD_SIZE)
    resid_mid = resid_in + jnp.dot(flat_att, output_all, preferred_element_type=jnp.float32)
    inv_two = lax.rsqrt(jnp.mean(resid_mid * resid_mid, axis=-1, keepdims=True) + eps)
    unit_two = resid_mid * inv_two
    normed_two = (unit_two * gain_two).astype(half_precision)
    gate = jnp.dot(normed_two, gate_all, preferred_element_type=jnp.float32)
    upward = jnp.dot(normed_two, up_all, preferred_element_type=jnp.float32)
    sigma = jax.nn.sigmoid(gate)
    silu_gate = gate * sigma
    hidden = (silu_gate * upward).astype(half_precision)
    layer_output = (
        resid_mid + jnp.dot(hidden, down_all, preferred_element_type=jnp.float32)
    ).astype(half_precision)
    upstream = cotangent.reshape(token_rows, width)
    grad_hidden = times_transposed(upstream, down_all)
    down_grad = transposed_times(hidden, upstream)
    grad_gate = (grad_hidden * upward * sigma * (1.0 + gate * (1.0 - sigma))).astype(half_precision)
    grad_up = (grad_hidden * silu_gate).astype(half_precision)
    gate_grad = transposed_times(normed_two, grad_gate)
    up_grad = transposed_times(normed_two, grad_up)
    grad_norm_two = times_transposed(grad_gate, gate_all) + times_transposed(grad_up, up_all)
    ffn_gain_grad = jnp.sum(grad_norm_two * unit_two, axis=0)
    gate_grad, up_grad, down_grad, ffn_gain_grad = (
        lax.psum_scatter(
            gate_grad.astype(jnp.bfloat16), "dp", scatter_dimension=0, tiled=True
        ).astype(jnp.float32),
        lax.psum_scatter(
            up_grad.astype(jnp.bfloat16), "dp", scatter_dimension=0, tiled=True
        ).astype(jnp.float32),
        lax.psum_scatter(
            down_grad.astype(jnp.bfloat16), "dp", scatter_dimension=0, tiled=True
        ).astype(jnp.float32),
        lax.psum_scatter(
            ffn_gain_grad.astype(jnp.bfloat16), "dp", scatter_dimension=0, tiled=True
        ).astype(jnp.float32),
    )
    gate_grad, up_grad, down_grad, ffn_gain_grad = (
        lax.psum(gate_grad.astype(jnp.bfloat16), "seq").astype(jnp.float32),
        lax.psum(up_grad.astype(jnp.bfloat16), "seq").astype(jnp.float32),
        lax.psum(down_grad.astype(jnp.bfloat16), "seq").astype(jnp.float32),
        lax.psum(ffn_gain_grad.astype(jnp.bfloat16), "seq").astype(jnp.float32),
    )
    grad_mid = upstream.astype(jnp.float32) + norm_backward(
        grad_norm_two, unit_two, gain_two, inv_two
    )
    grad_mid_half = grad_mid.astype(half_precision)
    out_grad = transposed_times(flat_att, grad_mid_half)
    grad_att = (
        times_transposed(grad_mid_half, output_all)
        .astype(half_precision)
        .reshape(sequence_count, local_length, query_group_count, KEY_VALUE_HEADS * HEAD_SIZE)
    )
    grad_heads = lax.all_to_all(grad_att, "seq", split_axis=3, concat_axis=1, tiled=True)
    grad_heads = grad_heads.reshape(
        sequence_count, length, query_group_count, local_key_value, HEAD_SIZE
    )
    query_grad_blocks = []
    key_gradient = jnp.zeros((sequence_count, length, local_key_value, HEAD_SIZE), jnp.float32)
    value_gradient = jnp.zeros((sequence_count, length, local_key_value, HEAD_SIZE), jnp.float32)
    for index in range(count):
        start_offset = index * block
        stop = start_offset + block
        query_block = query_heads[:, start_offset:stop]
        key_block = key_heads[:, :stop]
        value_block = value_heads[:, :stop]
        grad_block = grad_heads[:, start_offset:stop]
        probs, unused = block_probs(query_block, key_block, start_offset, logsums[index])
        probs_half = probs.astype(half_precision)
        grad_probs = jnp.einsum(
            "sqgcd,skcd->sgcqk", grad_block, value_block, preferred_element_type=jnp.float32
        )
        delta = jnp.sum(
            grad_block.astype(jnp.float32)
            * attended_heads[:, start_offset:stop].astype(jnp.float32),
            axis=-1,
        )
        delta = jnp.transpose(delta, (0, 2, 3, 1))[..., None]
        grad_scores = (probs * (grad_probs - delta)).astype(half_precision)
        query_grad_blocks.append(
            jnp.einsum(
                "sgcqk,skcd->sqgcd", grad_scores, key_block, preferred_element_type=jnp.float32
            )
            * scale
        )
        key_part = (
            jnp.einsum(
                "sgcqk,sqgcd->skcd", grad_scores, query_block, preferred_element_type=jnp.float32
            )
            * scale
        )
        value_part = jnp.einsum(
            "sgcqk,sqgcd->skcd", probs_half, grad_block, preferred_element_type=jnp.float32
        )
        padding = ((0, 0), (0, length - stop), (0, 0), (0, 0))
        key_gradient = key_gradient + jnp.pad(key_part, padding)
        value_gradient = value_gradient + jnp.pad(value_part, padding)
    grad_queries = jnp.concatenate(query_grad_blocks, axis=1)
    cos_full, sin_full = rope_tables(length, 0, HEAD_SIZE)
    queries_back = rotary_backward(
        grad_queries, cos_full[:, None, None, :], sin_full[:, None, None, :]
    ).astype(half_precision)
    key_rows_restored = rotary_backward(
        key_gradient, cos_full[:, None, :], sin_full[:, None, :]
    ).astype(half_precision)
    value_rows_restored = value_gradient.astype(half_precision)
    queries_back = queries_back.reshape(
        sequence_count, length, query_group_count, local_key_value * HEAD_SIZE
    )
    pair_back = jnp.stack(
        [
            key_rows_restored.reshape(sequence_count, length, local_key_value * HEAD_SIZE),
            value_rows_restored.reshape(sequence_count, length, local_key_value * HEAD_SIZE),
        ],
        axis=2,
    )
    queries_tok, paired_token_rows = (
        lax.all_to_all(queries_back, "seq", split_axis=1, concat_axis=3, tiled=True),
        lax.all_to_all(pair_back, "seq", split_axis=1, concat_axis=3, tiled=True),
    )
    queries_tok = queries_tok.reshape(token_rows, QUERY_HEADS * HEAD_SIZE)
    key_token_rows = paired_token_rows[:, :, 0].reshape(token_rows, KEY_VALUE_HEADS * HEAD_SIZE)
    value_token_rows = paired_token_rows[:, :, 1].reshape(token_rows, KEY_VALUE_HEADS * HEAD_SIZE)
    query_grad = transposed_times(first_normed, queries_tok)
    key_grad = transposed_times(first_normed, key_token_rows)
    value_grad = transposed_times(first_normed, value_token_rows)
    grad_norm_one = (
        times_transposed(queries_tok, query_all)
        + times_transposed(key_token_rows, key_all)
        + times_transposed(value_token_rows, value_all)
    )
    attn_gain_grad = jnp.sum(grad_norm_one * unit_one, axis=0)
    query_grad, key_grad, value_grad, out_grad, attn_gain_grad = (
        lax.psum_scatter(
            query_grad.astype(jnp.bfloat16), "dp", scatter_dimension=0, tiled=True
        ).astype(jnp.float32),
        lax.psum_scatter(
            key_grad.astype(jnp.bfloat16), "dp", scatter_dimension=0, tiled=True
        ).astype(jnp.float32),
        lax.psum_scatter(
            value_grad.astype(jnp.bfloat16), "dp", scatter_dimension=0, tiled=True
        ).astype(jnp.float32),
        lax.psum_scatter(
            out_grad.astype(jnp.bfloat16), "dp", scatter_dimension=0, tiled=True
        ).astype(jnp.float32),
        lax.psum_scatter(
            attn_gain_grad.astype(jnp.bfloat16), "dp", scatter_dimension=0, tiled=True
        ).astype(jnp.float32),
    )
    query_grad, key_grad, value_grad, out_grad, attn_gain_grad = (
        lax.psum(query_grad.astype(jnp.bfloat16), "seq").astype(jnp.float32),
        lax.psum(key_grad.astype(jnp.bfloat16), "seq").astype(jnp.float32),
        lax.psum(value_grad.astype(jnp.bfloat16), "seq").astype(jnp.float32),
        lax.psum(out_grad.astype(jnp.bfloat16), "seq").astype(jnp.float32),
        lax.psum(attn_gain_grad.astype(jnp.bfloat16), "seq").astype(jnp.float32),
    )
    input_grad = grad_mid + norm_backward(grad_norm_one, unit_one, gain_one, inv_one)
    return (
        layer_output.reshape(sequence_count, local_length, width),
        input_grad.reshape(sequence_count, local_length, width),
        attn_gain_grad,
        query_grad,
        key_grad,
        value_grad,
        out_grad,
        ffn_gain_grad,
        gate_grad,
        up_grad,
        down_grad,
    )


SAME_CORE = [[0, 2, 4, 6], [1, 3, 5, 7]]
VMEM_BYTES = 48 * 1024 * 1024


def flip(field, bit):
    count = lax.axis_size("dp")
    return lax.ppermute(field, "dp", [(i, i ^ bit) for i in range(count)])


def cross(field, bit):
    return lax.ppermute(field, "seq", [(i, i ^ bit) for i in range(4)])


def column_swap(field, turn, back):
    pairs = []
    for dp in range(8):
        for place in range(4):
            chip, core, high, low = dp // 2, dp % 2, place // 2, place % 2
            target = (2 * chip + (high ^ 1)) * 4 + 2 * core + (low ^ turn)
            pairs.append((target, dp * 4 + place) if back else (dp * 4 + place, target))
    return lax.ppermute(field, ("dp", "seq"), pairs)


def pick_order(swapped, first, second, axis=0):
    return jnp.where(
        swapped,
        jnp.concatenate([second, first], axis=axis),
        jnp.concatenate([first, second], axis=axis),
    )


def sequence_parts(field, low):
    return [
        column_swap(lax.dynamic_index_in_dim(field, low ^ turn, 0, keepdims=False), turn, False)
        for turn in range(2)
    ]


def slice_parts(half, low):
    rows = half.shape[0] // 2
    return [
        column_swap(lax.dynamic_slice_in_dim(half, (low ^ turn) * rows, rows, 0), turn, True)
        for turn in range(2)
    ]


def join_slices(parts, low):
    return jnp.where(low == 1, jnp.stack(parts[::-1]), jnp.stack(parts))


def both_cores(half, core):
    return pick_order(core == 0, half, flip(half, 1))


def relative_columns(field, chip):
    width = field.shape[-1] // 4
    return jnp.concatenate(
        [lax.dynamic_slice_in_dim(field, (chip ^ r) * width, width, field.ndim - 1) for r in range(4)],
        axis=-1,
    )


def gather_chips(block):
    half = block.shape[0] // 2
    from_x = flip(block, 2)
    from_y = flip(block, 4)
    corner_x = flip(from_y[:half], 2)
    corner_y = flip(from_x[half:], 4)
    return block, from_x, from_y, corner_x, corner_y


def add_half(*terms):
    total = terms[0].astype(jnp.float32)
    for term in terms[1:]:
        total = total + term.astype(jnp.float32)
    return total.astype(jnp.bfloat16)


def scatter_first(field):
    half = field.shape[0] // 8
    corner = field[6 * half :]
    return flip(corner[:half], 2), flip(corner[half:], 4)


def scatter_second(field, got_x, got_y):
    rows = field.shape[0] // 4
    half = rows // 2
    over_x, over_y = field[rows : 2 * rows], field[2 * rows : 3 * rows]
    send_x = jnp.concatenate([over_x[:half], add_half(over_x[half:], got_y)], axis=0)
    send_y = jnp.concatenate([add_half(over_y[:half], got_x), over_y[half:]], axis=0)
    return flip(send_x, 2), flip(send_y, 4)


def split_rows(field, which):
    size = field.shape[0] // 2
    own = lax.dynamic_slice_in_dim(field, which * size, size, 0)
    return own, lax.dynamic_slice_in_dim(field, (1 - which) * size, size, 0)


def prepare_kernel(core_ref, gate_mine, gate_theirs, up_mine, up_theirs, mine_ref, theirs_ref):
    for gate, up, out in ((gate_mine, up_mine, mine_ref), (gate_theirs, up_theirs, theirs_ref)):
        part = gate.shape[1] // 2
        for group in range(2):
            for offset, field in ((0, gate), (part, up)):
                start = 2 * part * group + offset
                out[:, start : start + part] = field[:, group * part : (group + 1) * part]


def prepare_ffn(gate_weight, up_weight, core):
    rows, columns = gate_weight.shape
    piece = columns // 8
    mine = pl.BlockSpec((rows, piece), lambda j, c: (0, 2 * j + c[0]))
    theirs = pl.BlockSpec((rows, piece), lambda j, c: (0, 2 * j + 1 - c[0]))
    out = pl.BlockSpec((rows, 2 * piece), lambda j, c: (0, j))
    shape = jax.ShapeDtypeStruct((rows, columns), jnp.bfloat16)
    return pl.pallas_call(
        prepare_kernel,
        out_shape=(shape, shape),
        grid_spec=pltpu.PrefetchScalarGridSpec(
            num_scalar_prefetch=1,
            grid=(4,),
            in_specs=[mine, theirs, mine, theirs],
            out_specs=(out, out),
        ),
        name="prepare_ffn",
    )(core.reshape(1), gate_weight, gate_weight, up_weight, up_weight)


def merge_kernel(core_ref, own_0, other_0, own_1, other_1, gate_ref, up_ref):
    part = own_0.shape[1] // 2
    mine = core_ref[0] == pl.program_id(1)
    first = jnp.where(mine, own_0[...].astype(jnp.float32), other_0[...].astype(jnp.float32))
    second = jnp.where(mine, own_1[...].astype(jnp.float32), other_1[...].astype(jnp.float32))
    gate_ref[:, :part] = first[:, :part]
    gate_ref[:, part:] = second[:, :part]
    up_ref[:, :part] = first[:, part:]
    up_ref[:, part:] = second[:, part:]


def merge_ffn(own_0, other_0, own_1, other_1, core):
    rows, columns = own_0.shape
    piece = columns // 4
    part = pl.BlockSpec((rows, piece), lambda j, i, c: (0, j))
    out = pl.BlockSpec((rows, piece), lambda j, i, c: (0, 2 * j + i))
    shape = jax.ShapeDtypeStruct((rows, columns * 2), jnp.float32)
    return pl.pallas_call(
        merge_kernel,
        out_shape=(shape, shape),
        grid_spec=pltpu.PrefetchScalarGridSpec(
            num_scalar_prefetch=1,
            grid=(4, 2),
            in_specs=[part] * 4,
            out_specs=(out, out),
        ),
        name="merge_ffn",
    )(core.reshape(1), own_0, other_0, own_1, other_1)


def hint(flops, bytes_accessed, transcendentals=0):
    return pl.CostEstimate(
        flops=flops // 64, transcendentals=transcendentals // 64, bytes_accessed=bytes_accessed // 64
    )


def stacked(pieces, rows):
    own, from_x, from_y, corner_x, corner_y = pieces
    rest = rows - corner_x.shape[0]
    return jnp.concatenate(
        [own[:rows, :], from_x[:rows, :], from_y[:rows, :], corner_x[...], corner_y[:rest, :]],
        axis=0,
    )


def hidden_kernel(rows, normed, upstream, *refs):
    down, hidden, grads = refs[5:]
    part = grads.shape[1] // 2
    weight = stacked(refs[:5], rows)
    tile = 256
    for start in range(0, normed.shape[0], tile):
        lines = pl.ds(start, tile)
        total = jnp.dot(normed[lines, :], weight, preferred_element_type=jnp.float32)
        grad_hidden = lax.dot_general(
            upstream[lines, :], down[...], (((1,), (1,)), ((), ())), preferred_element_type=jnp.float32
        )
        gate, upward = total[:, :part], total[:, part:]
        sigma = jax.nn.sigmoid(gate)
        silu_gate = gate * sigma
        hidden[lines, :] = (silu_gate * upward).astype(jnp.bfloat16)
        grads[lines, :part] = (
            grad_hidden * upward * sigma * (1.0 + gate * (1.0 - sigma))
        ).astype(jnp.bfloat16)
        grads[lines, part:] = (grad_hidden * silu_gate).astype(jnp.bfloat16)


def hidden_stage(normed, upstream, pieces, down, group):
    length, width = normed.shape
    columns = pieces[0].shape[1] // 2
    piece = columns // 4
    whole = pl.BlockSpec((length, width), lambda j: (0, 0), pipeline_mode=pl.Buffered(1))
    return pl.pallas_call(
        lambda *refs: hidden_kernel(width // 4, *refs),
        out_shape=(
            jax.ShapeDtypeStruct((length, columns // 2), jnp.bfloat16),
            jax.ShapeDtypeStruct((length, columns), jnp.bfloat16),
        ),
        grid=(4,),
        in_specs=[whole, whole]
        + [pl.BlockSpec((p.shape[0], piece), lambda j: (0, 2 * j + group)) for p in pieces]
        + [pl.BlockSpec((piece // 2, width), lambda j: (j, 0))],
        out_specs=(
            pl.BlockSpec((length, piece // 2), lambda j: (0, j)),
            pl.BlockSpec((length, piece), lambda j: (0, j)),
        ),
        compiler_params=pltpu.CompilerParams(vmem_limit_bytes=VMEM_BYTES),
        cost_estimate=hint(
            3 * length * width * columns,
            4 * length * width + 3 * width * columns + 3 * length * columns,
            length * columns // 2,
        ),
        name="hidden_stage",
    )(normed, upstream, *pieces, down)


NEGATIVE = -1e30
LANES = 128


def turned(field, cos, sin_low, sin_high, sign):
    half = HEAD_SIZE // 2
    spun = pltpu.roll(field, LANES - half, 1) * sin_low + pltpu.roll(field, half, 1) * sin_high
    return field * cos + sign * spun


def project_kernel(rows, heads, normed, cos, sin_low, sin_high, *refs):
    out, weight = refs[5:]
    own, from_x, from_y, corner_x, corner_y = refs[:5]
    rest = rows - corner_x.shape[0]

    @pl.when(pl.program_id(0) == 0)
    def _():
        start = 0
        for piece, count in (
            (own, rows), (from_x, rows), (from_y, rows), (corner_x, rows - rest), (corner_y, rest)
        ):
            lines = pl.ds(start, count)
            for head in range(heads):
                weight[lines, pl.ds(head * LANES, HEAD_SIZE)] = piece[
                    :count, pl.ds(head * HEAD_SIZE, HEAD_SIZE)
                ]
                weight[lines, pl.ds(head * LANES + HEAD_SIZE, LANES - HEAD_SIZE)] = jnp.zeros(
                    (count, LANES - HEAD_SIZE), jnp.bfloat16
                )
            start += count

    part = jnp.dot(normed[...], weight[...], preferred_element_type=jnp.float32)
    for head in range(heads):
        columns = slice(head * LANES, (head + 1) * LANES)
        field = part[:, columns]
        if head < heads * 3 // 4:
            field = turned(field, cos[...], sin_low[...], sin_high[...], 1.0)
        out[:, columns] = field.astype(jnp.bfloat16)


def project_stage(normed, pieces, tables):
    length, width = normed.shape
    columns = pieces[0].shape[1]
    heads = columns // HEAD_SIZE
    tile = 256
    table = pl.BlockSpec((tile, LANES), lambda i: (i, 0))
    rows, corner = width // 4, pieces[3].shape[0]
    counts = (rows, rows, rows, corner, rows - corner)
    return pl.pallas_call(
        lambda *refs: project_kernel(width // 4, heads, *refs),
        out_shape=(
            jax.ShapeDtypeStruct((length, heads * LANES), jnp.bfloat16),
            jax.ShapeDtypeStruct((width, heads * LANES), jnp.bfloat16),
        ),
        grid=(length // tile,),
        in_specs=[pl.BlockSpec((tile, width), lambda i: (i, 0)), table, table, table]
        + [
            pl.BlockSpec((count, columns), lambda i: (0, 0), pipeline_mode=pl.Buffered(1))
            for count in counts
        ],
        out_specs=(
            pl.BlockSpec((tile, heads * LANES), lambda i: (i, 0)),
            pl.BlockSpec((width, heads * LANES), lambda i: (0, 0), pipeline_mode=pl.Buffered(1)),
        ),
        compiler_params=pltpu.CompilerParams(vmem_limit_bytes=VMEM_BYTES),
        cost_estimate=hint(
            2 * length * width * heads * LANES,
            2 * length * width + 4 * width * columns + 2 * length * columns,
        ),
        name="project_stage",
    )(normed, *tables, *pieces)


def block_softmax(query, key, tile, index):
    scale = HEAD_SIZE ** (-0.5)
    lines = pl.ds(index * tile, tile)
    before = index * tile

    def scores(which):
        return scale * lax.dot_general(
            query[lines, :], key[which, :], (((1,), (1,)), ((), ())),
            preferred_element_type=jnp.float32,
        )

    last = scores(lines)
    seen = lax.broadcasted_iota(jnp.int32, (tile, tile), 0) >= lax.broadcasted_iota(
        jnp.int32, (tile, tile), 1
    )
    last = jnp.where(seen, last, NEGATIVE)
    peak = jnp.max(last, axis=1, keepdims=True)
    if before:
        earlier = scores(pl.ds(0, before))
        peak = jnp.maximum(peak, jnp.max(earlier, axis=1, keepdims=True))
    last = jnp.exp(last - peak)
    total = jnp.sum(last, axis=1, keepdims=True)
    if before:
        earlier = jnp.exp(earlier - peak)
        total = total + jnp.sum(earlier, axis=1, keepdims=True)
    inverse = 1.0 / total
    parts = [(lines, last * inverse)]
    if before:
        parts.append((pl.ds(0, before), earlier * inverse))
    return lines, parts


def attention_kernel(tile, query, key, value, out):
    for index in range(query.shape[0] // tile):
        lines, parts = block_softmax(query, key, tile, index)
        total = 0.0
        for which, probs in parts:
            total = total + jnp.dot(
                probs.astype(jnp.bfloat16), value[which, :], preferred_element_type=jnp.float32
            )
        out[lines, :] = total.astype(jnp.bfloat16)


def attention_stage(fields, heads, kv_heads):
    length = fields.shape[0]
    tile = min(256, length)
    spec = lambda start, count: pl.BlockSpec((length, LANES), lambda h: (0, start + h % count))
    return pl.pallas_call(
        lambda *refs: attention_kernel(tile, *refs),
        out_shape=jax.ShapeDtypeStruct((length, heads * LANES), jnp.bfloat16),
        grid=(heads,),
        in_specs=[spec(0, heads), spec(heads, kv_heads), spec(heads + kv_heads, kv_heads)],
        out_specs=spec(0, heads),
        compiler_params=pltpu.CompilerParams(vmem_limit_bytes=VMEM_BYTES),
        cost_estimate=hint(
            2 * heads * length * length * LANES,
            6 * heads * length * LANES,
            heads * length * length // 2,
        ),
        name="attention_stage",
    )(fields, fields, fields)


def attention_back_kernel(tile, *refs):
    query_0, query_1, key, value, out_0, out_1, grad_0, grad_1 = refs[:8]
    cos, sin_low, sin_high, back_0, back_1, key_back, value_back, key_sum, value_sum = refs[8:]
    scale = HEAD_SIZE ** (-0.5)
    key_sum[...] = jnp.zeros_like(key_sum)
    value_sum[...] = jnp.zeros_like(value_sum)
    for query, out, grad, back in (
        (query_0, out_0, grad_0, back_0),
        (query_1, out_1, grad_1, back_1),
    ):
        for index in range(query.shape[0] // tile):
            lines, parts = block_softmax(query, key, tile, index)
            upstream = grad[lines, :]
            delta = jnp.sum(
                upstream.astype(jnp.float32) * out[lines, :].astype(jnp.float32),
                axis=1,
                keepdims=True,
            )
            total = 0.0
            for which, probs in parts:
                grad_probs = lax.dot_general(
                    upstream, value[which, :], (((1,), (1,)), ((), ())),
                    preferred_element_type=jnp.float32,
                )
                grad_scores = (probs * (grad_probs - delta)).astype(jnp.bfloat16)
                total = total + jnp.dot(
                    grad_scores, key[which, :], preferred_element_type=jnp.float32
                )
                key_sum[which, :] += lax.dot_general(
                    grad_scores, query[lines, :], (((0,), (0,)), ((), ())),
                    preferred_element_type=jnp.float32,
                )
                value_sum[which, :] += lax.dot_general(
                    probs.astype(jnp.bfloat16), upstream, (((0,), (0,)), ((), ())),
                    preferred_element_type=jnp.float32,
                )
            back[lines, :] = turned(
                total * scale, cos[lines, :], sin_low[lines, :], sin_high[lines, :], -1.0
            ).astype(jnp.bfloat16)
    key_back[...] = turned(
        key_sum[...] * scale, cos[...], sin_low[...], sin_high[...], -1.0
    ).astype(jnp.bfloat16)
    value_back[...] = value_sum[...].astype(jnp.bfloat16)


def attention_back_stage(fields, attended, grads, tables, kv_heads):
    length = fields.shape[0]
    tile = min(256, length)
    spec = lambda start: pl.BlockSpec((length, LANES), lambda h: (0, start + h))
    table = pl.BlockSpec((length, LANES), lambda h: (0, 0))
    shape = jax.ShapeDtypeStruct((length, kv_heads * LANES), jnp.bfloat16)
    first, second = spec(0), spec(kv_heads)
    return pl.pallas_call(
        lambda *refs: attention_back_kernel(tile, *refs),
        out_shape=(shape,) * 4,
        grid=(kv_heads,),
        in_specs=[first, second, spec(2 * kv_heads), spec(3 * kv_heads)]
        + [first, second] * 2
        + [table] * 3,
        out_specs=(first,) * 4,
        scratch_shapes=[pltpu.VMEM((length, LANES), jnp.float32)] * 2,
        compiler_params=pltpu.CompilerParams(vmem_limit_bytes=VMEM_BYTES),
        cost_estimate=hint(
            10 * kv_heads * length * length * LANES,
            30 * kv_heads * length * LANES,
            kv_heads * length * length,
        ),
        name="attention_back_stage",
    )(fields, fields, fields, fields, attended, attended, grads, grads, *tables)


def inputs_back_kernel(rows, chip_ref, *refs):
    weight, field, out, sums = refs[-4:]
    columns = refs[0].shape[1]
    part = 0.0
    for j, grad in enumerate(refs[:-4]):
        part = part + lax.dot_general(
            grad[...], weight[:, j * columns : (j + 1) * columns], (((1,), (1,)), ((), ())),
            preferred_element_type=jnp.float32,
        )
    for r in range(4):
        where = pl.ds(pl.multiple_of((chip_ref[0] ^ r) * rows, 128), rows)
        out[:, where] = part[:, r * rows : (r + 1) * rows]
    total = field[...].astype(jnp.float32)
    unit = total * lax.rsqrt(jnp.mean(total * total, axis=1, keepdims=True) + eps)

    @pl.when(pl.program_id(0) == 0)
    def _():
        sums[...] = jnp.zeros_like(sums)

    sums[...] += jnp.sum((out[...] * unit).reshape(-1, 8, total.shape[1]), axis=0)


def inputs_back_stage(backs, weight, chip, field):
    length, columns = backs[0].shape
    width = weight.shape[0]
    tile = 256
    return pl.pallas_call(
        lambda *refs: inputs_back_kernel(width // 4, *refs),
        out_shape=(
            jax.ShapeDtypeStruct((length, width), jnp.float32),
            jax.ShapeDtypeStruct((8, width), jnp.float32),
        ),
        grid_spec=pltpu.PrefetchScalarGridSpec(
            num_scalar_prefetch=1,
            grid=(length // tile,),
            in_specs=[pl.BlockSpec((tile, columns), lambda i, c: (i, 0))] * len(backs)
            + [
                pl.BlockSpec(weight.shape, lambda i, c: (0, 0), pipeline_mode=pl.Buffered(1)),
                pl.BlockSpec((tile, width), lambda i, c: (i, 0)),
            ],
            out_specs=(
                pl.BlockSpec((tile, width), lambda i, c: (i, 0)),
                pl.BlockSpec((8, width), lambda i, c: (0, 0)),
            ),
        ),
        compiler_params=pltpu.CompilerParams(vmem_limit_bytes=VMEM_BYTES),
        cost_estimate=hint(
            2 * length * width * weight.shape[1], 2 * width * weight.shape[1] + 8 * length * width
        ),
        name="inputs_back_stage",
    )(chip.reshape(1), *backs, weight, field)


def norm_kernel(with_parts, chip_ref, field, *refs):
    total = field[...].astype(jnp.float32)
    if with_parts:
        part, other, gain, middle, out = refs
        total = total + part[...] + other[...].astype(jnp.float32)
        middle[...] = total
    else:
        gain, out = refs
    inverse = lax.rsqrt(jnp.mean(total * total, axis=1, keepdims=True) + eps)
    normed = (total * inverse * gain[...]).astype(jnp.bfloat16)
    width = total.shape[1] // 4
    for j in range(4):
        columns = pl.ds(pl.multiple_of((chip_ref[0] ^ j) * width, 128), width)
        out[:, columns] = normed[:, j * width : (j + 1) * width]


def norm_stage(field, gain, chip, *parts):
    length, width = field.shape
    tile = 256
    line = pl.BlockSpec((tile, width), lambda i, c: (i, 0))
    shapes = [jax.ShapeDtypeStruct((length, width), jnp.bfloat16)]
    if parts:
        shapes = [jax.ShapeDtypeStruct((length, width), jnp.float32)] + shapes
    return pl.pallas_call(
        lambda *refs: norm_kernel(len(parts) > 0, *refs),
        out_shape=tuple(shapes),
        grid_spec=pltpu.PrefetchScalarGridSpec(
            num_scalar_prefetch=1,
            grid=(length // tile,),
            in_specs=[line] * (1 + len(parts)) + [pl.BlockSpec((1, width), lambda i, c: (0, 0))],
            out_specs=(line,) * len(shapes),
        ),
        compiler_params=pltpu.CompilerParams(vmem_limit_bytes=VMEM_BYTES),
        cost_estimate=hint(16 * length * width, 12 * length * width),
        name="norm_stage",
    )(chip.reshape(1), field, *parts, gain[None])


def norm_back_kernel(grad, other, middle, upstream, gain, out, out_half, sums):
    total = middle[...]
    inverse = lax.rsqrt(jnp.mean(total * total, axis=1, keepdims=True) + eps)
    unit = total * inverse
    own = grad[...]
    scaled = (own + other[...].astype(jnp.float32)) * gain[...]
    average = jnp.mean(scaled * unit, axis=1, keepdims=True)
    result = upstream[...].astype(jnp.float32) + inverse * (scaled - unit * average)
    out[...] = result
    out_half[...] = result.astype(jnp.bfloat16)

    @pl.when(pl.program_id(0) == 0)
    def _():
        sums[...] = jnp.zeros_like(sums)

    sums[...] += jnp.sum((own * unit).reshape(-1, 8, own.shape[1]), axis=0)


def norm_back_stage(grad, other, middle, upstream, gain):
    length, width = grad.shape
    tile = 256
    line = pl.BlockSpec((tile, width), lambda i: (i, 0))
    return pl.pallas_call(
        norm_back_kernel,
        out_shape=(
            jax.ShapeDtypeStruct((length, width), jnp.float32),
            jax.ShapeDtypeStruct((length, width), jnp.bfloat16),
            jax.ShapeDtypeStruct((8, width), jnp.float32),
        ),
        grid=(length // tile,),
        in_specs=[line] * 4 + [pl.BlockSpec((1, width), lambda i: (0, 0))],
        out_specs=(line, line, pl.BlockSpec((8, width), lambda i: (0, 0))),
        compiler_params=pltpu.CompilerParams(vmem_limit_bytes=VMEM_BYTES),
        cost_estimate=hint(16 * length * width, 18 * length * width),
        name="norm_back_stage",
    )(grad, other, middle, upstream, gain[None])


def outer_kernel(left, right, out):
    out[...] = lax.dot_general(
        left[...], right[...], (((0,), (0,)), ((), ())), preferred_element_type=jnp.float32
    ).astype(jnp.bfloat16)


def outer_stage(left, right):
    length, rows = left.shape
    columns = right.shape[1]
    tile = 256
    return pl.pallas_call(
        outer_kernel,
        out_shape=jax.ShapeDtypeStruct((rows, columns), jnp.bfloat16),
        grid=(rows // tile,),
        in_specs=[
            pl.BlockSpec((length, tile), lambda i: (0, i)),
            pl.BlockSpec((length, columns), lambda i: (0, 0), pipeline_mode=pl.Buffered(1)),
        ],
        out_specs=pl.BlockSpec((tile, columns), lambda i: (i, 0)),
        compiler_params=pltpu.CompilerParams(vmem_limit_bytes=VMEM_BYTES),
        cost_estimate=hint(2 * length * rows * columns, 2 * (rows + columns) * length),
        name="outer_stage",
    )(left, right)


def down_kernel(hidden_0, hidden_1, down_0, down_1, out):
    out[...] = jnp.dot(
        hidden_0[...], down_0[...], preferred_element_type=jnp.float32
    ) + jnp.dot(hidden_1[...], down_1[...], preferred_element_type=jnp.float32)


def down_stage(hidden_0, hidden_1, down_0, down_1):
    length, units = hidden_0.shape
    width = down_0.shape[1]
    tile = 256
    line = pl.BlockSpec((tile, units), lambda i: (i, 0))
    whole = pl.BlockSpec((units, width), lambda i: (0, 0), pipeline_mode=pl.Buffered(1))
    return pl.pallas_call(
        down_kernel,
        out_shape=jax.ShapeDtypeStruct((length, width), jnp.float32),
        grid=(length // tile,),
        in_specs=[line, line, whole, whole],
        out_specs=pl.BlockSpec((tile, width), lambda i: (i, 0)),
        compiler_params=pltpu.CompilerParams(vmem_limit_bytes=VMEM_BYTES),
        cost_estimate=hint(4 * length * units * width, 4 * units * (length + width)),
        name="down_stage",
    )(hidden_0, hidden_1, down_0, down_1)


def output_back_kernel(grad, attended, weight, out, weight_grad, total):
    step = pl.program_id(0)
    out[...] = lax.dot_general(
        grad[...], weight[...], (((1,), (1,)), ((), ())), preferred_element_type=jnp.float32
    ).astype(jnp.bfloat16)
    part = lax.dot_general(
        attended[...], grad[...], (((0,), (0,)), ((), ())), preferred_element_type=jnp.float32
    )

    @pl.when(step == 0)
    def _():
        total[...] = part

    @pl.when(step > 0)
    def _():
        total[...] += part

    @pl.when(step == pl.num_programs(0) - 1)
    def _():
        for head in range(total.shape[0] // LANES):
            weight_grad[pl.ds(head * HEAD_SIZE, HEAD_SIZE), :] = total[
                pl.ds(head * LANES, HEAD_SIZE), :
            ].astype(jnp.bfloat16)


def output_back_stage(grad, attended, weight):
    length, width = grad.shape
    columns = attended.shape[1]
    rows = columns // LANES * HEAD_SIZE
    tile = 512
    return pl.pallas_call(
        output_back_kernel,
        out_shape=(
            jax.ShapeDtypeStruct((length, columns), jnp.bfloat16),
            jax.ShapeDtypeStruct((rows, width), jnp.bfloat16),
        ),
        grid=(length // tile,),
        in_specs=[
            pl.BlockSpec((tile, width), lambda i: (i, 0)),
            pl.BlockSpec((tile, columns), lambda i: (i, 0)),
            pl.BlockSpec((columns, width), lambda i: (0, 0), pipeline_mode=pl.Buffered(1)),
        ],
        out_specs=(
            pl.BlockSpec((tile, columns), lambda i: (i, 0)),
            pl.BlockSpec((rows, width), lambda i: (0, 0), pipeline_mode=pl.Buffered(1)),
        ),
        scratch_shapes=[pltpu.VMEM((columns, width), jnp.float32)],
        compiler_params=pltpu.CompilerParams(vmem_limit_bytes=VMEM_BYTES),
        cost_estimate=hint(4 * length * width * columns, 4 * width * (length + columns)),
        name="output_back_stage",
    )(grad, attended, weight)


def weight_kernel(normed, *refs):
    gains, out = refs[-2:]
    rows = normed.shape[1]
    heads = refs[0].shape[1] // LANES
    for j, back in enumerate(refs[:-2]):
        part = lax.dot_general(
            normed[...], back[...], (((0,), (0,)), ((), ())), preferred_element_type=jnp.float32
        ).astype(jnp.bfloat16)
        for head in range(heads):
            out[:rows, pl.ds((j * heads + head) * HEAD_SIZE, HEAD_SIZE)] = part[
                :, head * LANES : head * LANES + HEAD_SIZE
            ]
    out[rows:, :] = gains[...]


def weight_stage(normed, backs, gains):
    length, width = normed.shape
    columns = gains.shape[1]
    rows, extra = width // 4, gains.shape[0] // 4
    whole = pl.BlockSpec(backs[0].shape, lambda i: (0, 0), pipeline_mode=pl.Buffered(1))
    return pl.pallas_call(
        weight_kernel,
        out_shape=jax.ShapeDtypeStruct((width + 4 * extra, columns), jnp.bfloat16),
        grid=(4,),
        in_specs=[pl.BlockSpec((length, rows), lambda i: (0, i))]
        + [whole] * len(backs)
        + [pl.BlockSpec((extra, columns), lambda i: (i, 0))],
        out_specs=pl.BlockSpec((rows + extra, columns), lambda i: (i, 0)),
        compiler_params=pltpu.CompilerParams(vmem_limit_bytes=VMEM_BYTES),
        cost_estimate=hint(
            2 * length * width * columns,
            2 * length * width + 2 * width * columns + 2 * length * columns,
        ),
        name="weight_stage",
    )(normed, *backs, gains)


def back_kernel(rows, with_base, chip_ref, grads, *rest):
    weight, out = rest[-1], rest[-2]
    piece = rest[0].shape[1]

    @pl.when(pl.program_id(0) == 0)
    def _():
        for j in range(4):
            start = 0
            for part in rest[5 * j : 5 * j + 5]:
                count = part.shape[0]
                weight[start : start + count, j * piece : (j + 1) * piece] = part[...]
                start += count

    part = lax.dot_general(
        grads[...], weight[...], (((1,), (1,)), ((), ())), preferred_element_type=jnp.float32
    )
    for r in range(4):
        columns = pl.ds(pl.multiple_of((chip_ref[0] ^ r) * rows, 128), rows)
        block = part[:, r * rows : (r + 1) * rows]
        if with_base:
            block = block + rest[20][:, columns]
        out[:, columns] = block


def back_stage(grads, pieces, chip, group, base=None):
    length, columns = grads.shape
    width = pieces[0].shape[0] * 4
    piece = columns // 4
    tile = 256
    line = pl.BlockSpec((tile, width), lambda i, c: (i, 0))

    def part_spec(rows, j):
        return pl.BlockSpec(
            (rows, piece), lambda i, c: (0, 2 * j + group), pipeline_mode=pl.Buffered(1)
        )

    inputs = [grads, *(list(pieces) * 4)] + ([] if base is None else [base])
    return pl.pallas_call(
        lambda *refs: back_kernel(width // 4, base is not None, *refs),
        out_shape=jax.ShapeDtypeStruct((length, width), jnp.float32),
        grid_spec=pltpu.PrefetchScalarGridSpec(
            num_scalar_prefetch=1,
            grid=(length // tile,),
            in_specs=[pl.BlockSpec((tile, columns), lambda i, c: (i, 0))]
            + [part_spec(p.shape[0], j) for j in range(4) for p in pieces]
            + ([] if base is None else [line]),
            out_specs=line,
            scratch_shapes=[pltpu.VMEM((width, columns), jnp.bfloat16)],
        ),
        compiler_params=pltpu.CompilerParams(vmem_limit_bytes=VMEM_BYTES),
        cost_estimate=hint(
            2 * length * width * columns,
            2 * length * columns + 2 * width * columns + 4 * length * width,
        ),
        name="back_stage",
    )(chip.reshape(1), *inputs)


def split_cores(field, chips):
    piece = field.shape[1] // (2 * chips)
    cuts = [field[:, i * piece : (i + 1) * piece] for i in range(2 * chips)]
    return cuts[::2], cuts[1::2]


def interleave(own, other, chips, core):
    piece = own.shape[1] // chips
    parts = []
    for i in range(chips):
        a, b = own[:, i * piece : (i + 1) * piece], other[:, i * piece : (i + 1) * piece]
        parts += [jnp.where(core == 0, a, b), jnp.where(core == 0, b, a)]
    return jnp.concatenate(parts, axis=1).astype(jnp.float32)


def paired_body(
    layer_input,
    attn_gain,
    query_weight,
    key_matrix,
    value_matrix,
    output_weight,
    ffn_gain,
    gate_weight,
    up_weight,
    down_weight,
    cotangent,
):
    f32, bf16 = jnp.float32, jnp.bfloat16
    sequence_count, local_length, width = layer_input.shape
    place = lax.axis_index("seq")
    dp = lax.axis_index("dp")
    core, chip, low = dp % 2, dp // 2, place % 2
    length = local_length * 4
    tokens = length // 2
    kv_heads = KEY_VALUE_HEADS // 2
    groups = QUERY_HEADS // KEY_VALUE_HEADS
    kv_width = kv_heads * HEAD_SIZE

    def half_rows(field):
        return lax.dynamic_slice_in_dim(field, (1 - core) * tokens, tokens, 0)

    def other_rows(field):
        return lax.dynamic_slice_in_dim(field, core * tokens, tokens, 0)

    def chain(token, *fields):
        return lax.optimization_barrier((token,) + fields)

    token = layer_input[0, 0, :8]
    core_rows = query_weight.shape[0]
    chip_rows = 2 * core_rows

    own_gains = jnp.concatenate(
        [attn_gain, ffn_gain, jnp.zeros((width - 2 * core_rows,), bf16)]
    )
    own_gains = jnp.pad(own_gains[None], ((0, 7), (0, 0)))
    even, odd = [], []
    for field, chips in ((query_weight, 4), (key_matrix, 2), (value_matrix, 2)):
        first, second = split_cores(field, chips)
        even, odd = even + first, odd + second
    even, odd = jnp.concatenate(even, axis=1), jnp.concatenate(odd, axis=1)
    mine, theirs = jnp.where(core == 0, even, odd), jnp.where(core == 0, odd, even)
    theirs = flip(jnp.concatenate([theirs, own_gains], axis=0), 1)
    both_parts = sequence_parts(jnp.concatenate([layer_input, cotangent], axis=1), low)
    theirs, their_gains = theirs[:core_rows], theirs[core_rows:]
    attn_block = jnp.where(
        core == 0,
        jnp.concatenate([mine, theirs, own_gains, their_gains], axis=0),
        jnp.concatenate([theirs, mine, their_gains, own_gains], axis=0),
    )
    part_rows = down_weight.shape[0] // 2
    share = part_rows // 4
    down_quarters = [
        lax.dynamic_slice_in_dim(down_weight, g * part_rows + place * share, share, 0)
        for g in range(2)
    ]
    attn_block = jnp.concatenate([attn_block, output_weight, *down_quarters], axis=0)
    cut = attn_block.shape[0] // 32 * 16
    attn_x, attn_y = flip(attn_block, 2), flip(attn_block, 4)
    ffn_mine, ffn_theirs = prepare_ffn(gate_weight, up_weight, core)
    ffn_other = flip(ffn_theirs, 1)
    ffn_block = pick_order(core == 1, ffn_mine, ffn_other)
    token, attn_x, attn_y = chain(token, attn_x, attn_y)
    corner_x, corner_y = flip(attn_y[:cut], 2), flip(attn_x[cut:], 4)
    token, corner_x, corner_y, ffn_block = chain(token, corner_x, corner_y, ffn_block)
    ffn_sides = (flip(ffn_block, 2), flip(ffn_block, 4))
    token, *both_parts = chain(token, *both_parts)
    halves = [p.reshape(2, local_length, width) for p in both_parts]
    here = pick_order(low == 1, *halves, axis=1)
    there = flip(here, 1)
    both = pick_order(core == 0, here, there, axis=1)
    inputs_full, upstream = both[0], both[1]


    attn_pieces = (attn_block, attn_x, attn_y, corner_x, corner_y)
    extras = [p[-(16 + core_rows + 2 * share) :] for p in (attn_block, attn_x, attn_y, corner_y)]
    gains = jnp.concatenate(
        [g[i, :chip_rows].reshape(2, core_rows) for g in extras for i in (0, 8)], axis=1
    )

    def chip_order(start, count):
        field = jnp.stack([g[start : start + count] for g in extras])
        return jnp.concatenate(
            [lax.dynamic_index_in_dim(field, chip ^ r, 0, keepdims=False) for r in range(4)], axis=0
        )

    def share_quarters(field):
        whole = lax.all_gather(field, "seq", axis=0)
        return jnp.swapaxes(whole.reshape(4, 4, share, width), 0, 1).reshape(-1, width)

    output_all = chip_order(16, core_rows)
    down_0 = share_quarters(chip_order(16 + core_rows, share))
    down_1 = share_quarters(chip_order(16 + core_rows + share, share))
    gains = relative_columns(gains, chip).astype(f32)
    gain_one, gain_two = gains[0], gains[1]
    (first_normed,) = norm_stage(inputs_full, gain_one, chip)
    cosine_table, sine_table = rope_tables(length, 0, HEAD_SIZE)
    rest = ((0, 0), (0, LANES - HEAD_SIZE))
    first_half = jnp.arange(HEAD_SIZE)[None, :] < HEAD_SIZE // 2
    tables = (
        jnp.pad(cosine_table, rest),
        jnp.pad(jnp.where(first_half, -sine_table, 0.0), rest),
        jnp.pad(jnp.where(first_half, 0.0, sine_table), rest),
    )
    heads = groups * kv_heads
    fields, attn_weight = project_stage(first_normed, attn_pieces, tables)
    attended = attention_stage(fields, heads, kv_heads)
    token, attended, ffn_x, ffn_y = chain(token, attended, *ffn_sides)
    half = ffn_block.shape[0] // 2
    ffn_corners = (flip(ffn_y[:half], 2), flip(ffn_x[half:], 4))
    output_all = jnp.pad(
        output_all.reshape(heads, HEAD_SIZE, width), ((0, 0), (0, LANES - HEAD_SIZE), (0, 0))
    ).reshape(heads * LANES, width)
    attn_part = jnp.dot(attended, output_all, preferred_element_type=f32)
    attn_flip = flip(attn_part.astype(bf16), 1)
    token, attn_flip = chain(token, attn_flip)
    resid_mid, normed_two = norm_stage(inputs_full, gain_two, chip, attn_part, attn_flip)

    def scatter_down(field):
        return lax.psum_scatter(
            field, "dp", scatter_dimension=0, tiled=True, axis_index_groups=SAME_CORE
        )

    token, normed_two, down_0, *ffn_corners = chain(token, normed_two, down_0, *ffn_corners)
    ffn_pieces = (ffn_block, ffn_x, ffn_y, *ffn_corners)
    hidden_0, grads_0 = hidden_stage(normed_two, upstream, ffn_pieces, down_0, 0)
    token, grads_0, hidden_0 = chain(token, grads_0, hidden_0)
    ffn_grad_0 = outer_stage(normed_two, grads_0)
    token, grads_0, ffn_grad_0 = chain(token, grads_0, ffn_grad_0)
    first_0 = scatter_first(ffn_grad_0)
    grad_norm = back_stage(grads_0, ffn_pieces, chip, 0)
    token, grad_norm, hidden_0 = chain(token, grad_norm, hidden_0)
    down_grad_0 = outer_stage(hidden_0, upstream)
    token, down_grad_0, normed_two, down_1, *first_0 = chain(
        token, down_grad_0, normed_two, down_1, *first_0
    )
    second_0 = scatter_second(ffn_grad_0, *first_0)
    down_grad_0 = scatter_down(down_grad_0)
    hidden_1, grads_1 = hidden_stage(normed_two, upstream, ffn_pieces, down_1, 1)
    token, grads_1, hidden_1 = chain(token, grads_1, hidden_1)
    ffn_grad_1 = outer_stage(normed_two, grads_1)
    token, grads_1, ffn_grad_1 = chain(token, grads_1, ffn_grad_1)
    first_1 = scatter_first(ffn_grad_1)
    grad_norm = back_stage(grads_1, ffn_pieces, chip, 1, grad_norm)
    token, grad_norm, hidden_1 = chain(token, grad_norm, hidden_1)
    norm_flip = flip(grad_norm.astype(bf16), 1)
    down_grad_1 = outer_stage(hidden_1, upstream)
    token, down_grad_1, hidden_1, *second_0 = chain(token, down_grad_1, hidden_1, *second_0)
    ffn_sum_0 = add_half(ffn_grad_0[:chip_rows], *second_0)
    own_0, other_0 = split_rows(ffn_sum_0, low)
    near_0 = cross(other_0, 1)
    down_total = down_stage(hidden_0, hidden_1, down_0, down_1)
    token, down_grad_0, down_grad_1, down_total, grad_norm, norm_flip, near_0, *first_1 = chain(
        token, down_grad_0, down_grad_1, down_total, grad_norm, norm_flip, near_0, *first_1
    )
    second_1 = scatter_second(ffn_grad_1, *first_1)
    down_grad_1 = scatter_down(down_grad_1)
    pair_0 = add_half(own_0, near_0)
    far_0 = cross(pair_0, 2)
    down_flip = flip(other_rows(down_total).astype(bf16), 1)
    grad_mid, grad_mid_half, gain_sums_two = norm_back_stage(
        grad_norm, norm_flip, resid_mid, upstream, gain_two
    )
    ffn_gain_grad = jnp.sum(gain_sums_two, axis=0)
    token, grad_mid_half, down_flip = chain(token, grad_mid_half, down_flip)
    layer_half = (half_rows(resid_mid + down_total) + down_flip.astype(f32)).astype(bf16)
    grad_att, out_grad = output_back_stage(grad_mid_half, attended, output_all)
    token, grad_att, out_grad, layer_half, far_0 = chain(
        token, grad_att, out_grad, layer_half, far_0
    )
    out_grad = scatter_down(out_grad)
    total_0 = add_half(pair_0, far_0)
    last_0 = cross(total_0, 1)
    layer_parts = slice_parts(layer_half, low)
    backs = attention_back_stage(fields, attended, grad_att, tables, kv_heads)
    token, last_0, down_grad_1, *rest = chain(
        token, last_0, down_grad_1, *second_1, *layer_parts, *backs
    )
    second_1, layer_parts, backs = rest[:2], rest[2:4], rest[4:]
    ffn_sum_1 = add_half(ffn_grad_1[:chip_rows], *second_1)
    own_1, other_1 = split_rows(ffn_sum_1, low)
    near_1 = cross(other_1, 1)
    part_one, gain_sums_one = inputs_back_stage(backs, attn_weight, chip, inputs_full)
    attn_gain_grad = jnp.sum(gain_sums_one, axis=0)
    gain_grads = relative_columns(jnp.stack([attn_gain_grad, ffn_gain_grad]), chip).astype(bf16)
    gain_grads = jnp.transpose(gain_grads.reshape(2, 8, core_rows), (1, 0, 2))
    gain_grads = jnp.pad(
        gain_grads.reshape(8, 1, chip_rows), ((0, 0), (0, 7), (0, width - chip_rows))
    ).reshape(64, width)
    token, gain_grads, part_one, out_grad, near_1 = chain(
        token, gain_grads, part_one, out_grad, near_1
    )
    row_sum = lax.psum(jnp.concatenate([down_grad_0, down_grad_1, out_grad], axis=0), "seq")
    pair_1 = add_half(own_1, near_1)
    far_1 = cross(pair_1, 2)
    attn_grad = weight_stage(first_normed, backs, gain_grads)
    token, attn_grad, part_one = chain(token, attn_grad, part_one)
    first_2 = scatter_first(attn_grad)
    part_flip = flip(other_rows(part_one).astype(bf16), 1)
    layer_output = join_slices(layer_parts, low)
    ffn_sum_0 = pick_order(low == 1, total_0, last_0)
    token, layer_output, ffn_sum_0, part_flip, far_1, *first_2 = chain(
        token, layer_output, ffn_sum_0, part_flip, far_1, *first_2
    )
    second_2 = scatter_second(attn_grad, *first_2)
    total_1 = add_half(pair_1, far_1)
    last_1 = cross(total_1, 1)
    grad_norm_one = half_rows(part_one) + part_flip.astype(f32)
    resid_in = half_rows(inputs_full).astype(f32)
    inverse = lax.rsqrt(jnp.mean(resid_in * resid_in, axis=-1, keepdims=True) + eps)
    input_grad = half_rows(grad_mid) + norm_backward(
        grad_norm_one, resid_in * inverse, gain_one, inverse
    )
    token, input_grad, last_1, *second_2 = chain(token, input_grad, last_1, *second_2)
    attn_grad = add_half(attn_grad[: chip_rows + 16], *second_2)
    tail_own, tail_other = split_rows(attn_grad, low)
    tail_near = cross(tail_other, 1)
    token, tail_near, row_sum = chain(token, tail_near, row_sum)
    tail = add_half(tail_own, tail_near)
    tail_far = cross(tail, 2)
    input_parts = slice_parts(input_grad.astype(bf16), low)
    token, tail_far = chain(token, tail_far)
    tail = add_half(tail, tail_far)
    tail_last = cross(tail, 1)
    ffn_sum_1 = pick_order(low == 1, total_1, last_1)

    def settle(field, size, extra=None):
        own = lax.dynamic_slice_in_dim(field, core * size, size, 0)
        other = lax.dynamic_slice_in_dim(field, (1 - core) * size, size, 0)
        if extra is not None:
            lines = extra.shape[0] // 2
            own = (own, lax.dynamic_slice_in_dim(extra, core * lines, lines, 0))
            other = jnp.concatenate(
                [other, lax.dynamic_slice_in_dim(extra, (1 - core) * lines, lines, 0)], axis=0
            )
        return own, flip(other, 1)

    settled = settle(ffn_sum_0, core_rows) + settle(ffn_sum_1, core_rows)
    token, *settled = chain(token, *settled)
    gate_grad, up_grad = merge_ffn(*settled, core)
    row_sum = row_sum.astype(f32)
    down_grad, out_grad = row_sum[: 2 * part_rows], row_sum[2 * part_rows :]
    token, tail_last, gate_grad, up_grad, down_grad, out_grad = chain(
        token, tail_last, gate_grad, up_grad, down_grad, out_grad
    )
    tail = pick_order(low == 1, tail, tail_last)
    (attn_own, gains_own), attn_other = settle(
        tail[:chip_rows], core_rows, tail[chip_rows:]
    )
    gain_sums = (
        0.0 * token[0].astype(f32)
        + gains_own[0, :chip_rows].astype(f32)
        + attn_other[core_rows, :chip_rows].astype(f32)
    )
    attn_other = attn_other[:core_rows]
    input_grad = join_slices(input_parts, low).astype(f32)
    cuts = (0, groups * kv_width, (groups + 1) * kv_width, (groups + 2) * kv_width)
    query_grad, key_grad, value_grad = [
        interleave(
            attn_own[:, cuts[i] : cuts[i + 1]], attn_other[:, cuts[i] : cuts[i + 1]], chips, core
        )
        for i, chips in enumerate((4, 2, 2))
    ]
    return (
        layer_output,
        input_grad,
        gain_sums[:core_rows],
        query_grad,
        key_grad,
        value_grad,
        out_grad,
        gain_sums[core_rows:],
        gate_grad,
        up_grad,
        down_grad,
    )


def any_body(layer_input, *rest):
    paired = (
        lax.axis_size("dp") == 8 and lax.axis_size("seq") == 4 and layer_input.shape[0] == 2
    )
    return (paired_body if paired else body)(layer_input, *rest)


def solution(mesh):
    return jax.shard_map(
        any_body,
        mesh=mesh,
        in_specs=(
            P("dp", "seq", None),
            P("dp"),
            P("dp", None),
            P("dp", None),
            P("dp", None),
            P("dp", None),
            P("dp"),
            P("dp", None),
            P("dp", None),
            P("dp", None),
            P("dp", "seq", None),
        ),
        out_specs=(
            P("dp", "seq", None),
            P("dp", "seq", None),
            P("dp"),
            P("dp", None),
            P("dp", None),
            P("dp", None),
            P("dp", None),
            P("dp"),
            P("dp", None),
            P("dp", None),
            P("dp", None),
        ),
        check_vma=False,
    )
```
